32 devices in a mesh: box: 16 (over z, y, x), dir: 2 (over core).
Axes of the slice: x: 2, y: 2, z: 4, core: 2. Of those that a mesh axis runs over, the one named last changes fastest.
Arguments:
- sources: bfloat16 [64, 2, 32, 256], P('box'), may hold values from -6 to 6
- encode: bfloat16 [2, 1024, 256], P(None, 'dir'), may hold values from -0.375 to 0.375
- kernel: float32 [1024, 2, 4, 128], P(('dir', 'box')), may hold values from -0.5 to 0.5
- decode: bfloat16 [2, 1024, 256], P(None, 'dir'), may hold values from -0.1875 to 0.1875
- near_blocks: bfloat16 [64, 28, 2, 256, 256], P('box', 'dir'), may hold values from -0.078125 to 0.078125
- near_list: int32 [64, 28], P('box', 'dir'), may hold values from 0 to 63, as said below
- near_mask: int32 [64, 28], P('box', 'dir'), may hold values from 0 to 1, as said below
- box_cell: int32 [64], replicated, may hold values from 0 to 63, as said below
Outputs:
- product: float32 [64, 2, 32, 256], P('box', None, None, 'dir')
The draws below stay inside these ranges and needn't reach their ends.
Inputs may be any that keep to these rules, and one draw needn't show every extreme that they name: A permutation of the cells: box b lies in cell box_cell[b] = (ix * 8 + iy) * 4 + iz of the 2 x 8 x 4 grid. Where near_mask[b, s] is 1, near_list[b, s] is the box whose cell differs from box b's cell by -1, 0 or 1 along each dimension, each such box named in one slot of b (b itself included); elsewhere any box. `near_mask`: 1 exactly where the slot names a cell inside the grid; at least one slot of every box is 0.
All inputs are finite; a program needn't handle non-finite values.
Results may differ from the reference program's by a relative error of at most 0.0027.
Values may be sent and summed in bfloat16 or wider, within the bound.
No kernel may reach another device: no remote copies, remote signals or barrier semaphores. Data moves between devices by JAX's collectives and lax.ppermute only.
A program may use at most 128 MiB of HBM per device.

```python
import jax
import jax.numpy as jnp
from jax import lax

P_SIZE = 256
K = 1024
R = 32
SLOTS = 28
GY = 8
GZ = 4
BOXES = 64
GX = 2


def grid_layout(key):
    cells = jax.random.permutation(jax.random.fold_in(key, 101), BOXES).astype(jnp.int32)
    at_cell = jnp.zeros((BOXES,), jnp.int32).at[cells].set(jnp.arange(BOXES, dtype=jnp.int32))
    code = jnp.arange(27, dtype=jnp.int32)
    table = jnp.stack([code // 9 - 1, code // 3 % 3 - 1, code % 3 - 1], axis=1)
    filler = jnp.full((SLOTS - 27, 3), 2 * BOXES, jnp.int32)
    table = jnp.concatenate([table, filler], axis=0)
    box_keys = jax.random.split(jax.random.fold_in(key, 102), BOXES)
    orders = jax.vmap(lambda single: jax.random.permutation(single, SLOTS))(box_keys)
    stepped = table[orders]
    cell_x = cells // (GY * GZ)
    cell_y = cells // GZ % GY
    cell_z = cells % GZ
    next_x = cell_x[:, None] + stepped[:, :, 0]
    next_y = cell_y[:, None] + stepped[:, :, 1]
    next_z = cell_z[:, None] + stepped[:, :, 2]
    inside = (next_x >= 0) & (next_x < GX) & (next_y >= 0) & (next_y < GY) & (next_z >= 0) & (next_z < GZ)
    next_cell = (jnp.clip(next_x, 0, GX - 1) * GY + jnp.clip(next_y, 0, GY - 1)) * GZ + jnp.clip(next_z, 0, GZ - 1)
    filler_boxes = jax.random.randint(jax.random.fold_in(key, 103), (BOXES, SLOTS), 0, BOXES).astype(jnp.int32)
    neighbours = jnp.where(inside, at_cell[next_cell], filler_boxes).astype(jnp.int32)
    return (cells, neighbours, inside.astype(jnp.int32))


def draw_near_list(key, part):
    return grid_layout(key)[1]


def draw_near_mask(key, part):
    return grid_layout(key)[2]


def draw_box_cell(key, part):
    return grid_layout(key)[0]


def block_levels(key, shape, cuts, smallest, top_value):
    def one(dim, blocks):
        steps = jax.random.uniform(jax.random.fold_in(jax.random.fold_in(key, 6), dim), (blocks,), jnp.float32, smallest / len(cuts), top_value / len(cuts))
        return jnp.repeat(jnp.exp(steps), shape[dim] // blocks).reshape((-1,) + (1,) * (len(shape) - dim - 1))

    loudness = one(*cuts[0])
    for cut in cuts[1:]:
        loudness = loudness * one(*cut)
    return loudness


def bell_draw(own_key, dims, width, limit, cuts=(), kind=jnp.bfloat16):
    result = width * jax.random.normal(own_key, dims, jnp.float32)
    if cuts:
        result = result * block_levels(own_key, dims, cuts, -0.22, 0.18)
    return jnp.clip(result, -limit, limit).astype(kind)


def setup_inputs(seed: int = 0) -> dict:
    arg_keys = jax.random.split(jax.random.key(seed), 9)
    sources = bell_draw(arg_keys[0], (BOXES, 2, R, P_SIZE), 1.0, 6.0, ((0, 16),))
    encode = bell_draw(arg_keys[1], (2, K, P_SIZE), P_SIZE ** -0.5, 0.375, ((1, 2),))
    kernel = bell_draw(arg_keys[2], (K, 2, 2 * GX, 4 * GY * GZ), (2 * BOXES) ** -0.5, 0.5, ((0, 32),), jnp.float32)
    decode = bell_draw(arg_keys[3], (2, K, P_SIZE), K ** -0.5, 0.1875, ((1, 2),))
    near_blocks = bell_draw(arg_keys[4], (BOXES, SLOTS, 2, P_SIZE, P_SIZE), (27 * P_SIZE) ** -0.5, 0.078125, ((0, 16), (1, 2)))
    near_list = draw_near_list(jax.random.fold_in(arg_keys[8], 71), 0)
    near_mask = draw_near_mask(jax.random.fold_in(arg_keys[8], 71), 0)
    box_cell = draw_box_cell(jax.random.fold_in(arg_keys[8], 71), 0)
    return dict(sources=sources, encode=encode, kernel=kernel, decode=decode, near_blocks=near_blocks, near_list=near_list, near_mask=near_mask, box_cell=box_cell)


def near_line(length):
    halfway = length // 2
    index = jnp.arange(length, dtype=jnp.int32)
    offset = jnp.where(index < halfway, index, index - length)
    return jnp.abs(offset) <= 1


def keep_mask(double_x, double_y, double_z):
    near_x = near_line(double_x)
    near_plane = (near_line(double_y)[:, None] & near_line(double_z)[None, :]).reshape(-1)
    return jnp.where(near_x[:, None] & near_plane[None, :], 0.0, 1.0).astype(jnp.float32)


def contract_last(left, right):
    return lax.dot_general(left, right, (((1,), (1,)), ((), ())), preferred_element_type=jnp.float32)


def contract_first(left, right):
    return lax.dot_general(left, right, (((0,), (0,)), ((), ())), preferred_element_type=jnp.float32)


def reference(sources, encode, kernel, decode, near_blocks, near_list, near_mask, box_cell):
    flat_re = sources[:, 0].reshape(BOXES * R, P_SIZE)
    flat_im = sources[:, 1].reshape(BOXES * R, P_SIZE)
    coded_re = contract_last(encode[0], flat_re) - contract_last(encode[1], flat_im)
    coded_im = contract_last(encode[0], flat_im) + contract_last(encode[1], flat_re)
    coded = lax.complex(coded_re, coded_im).reshape(K, BOXES, R).transpose(0, 2, 1)
    placed = jnp.zeros((K, R, BOXES), coded.dtype).at[:, :, box_cell].set(coded)
    placed = placed.reshape(K, R, GX, GY, GZ)
    padded = jnp.pad(placed, ((0, 0), (0, 0), (0, GX), (0, GY), (0, GZ)))
    keep = keep_mask(2 * GX, 2 * GY, 2 * GZ)
    kern = lax.complex(kernel[:, 0] * keep, kernel[:, 1] * keep).reshape(K, 2 * GX, 2 * GY, 2 * GZ)
    spectrum = jnp.fft.fftn(padded, axes=(2, 3, 4)) * jnp.fft.fftn(kern, axes=(1, 2, 3))[:, None]
    far = jnp.fft.ifftn(spectrum, axes=(2, 3, 4))[:, :, :GX, :GY, :GZ].reshape(K, R, BOXES)
    far_box = far[:, :, box_cell]
    farb_re = jnp.real(far_box).astype(jnp.bfloat16).reshape(K, R * BOXES)
    farb_im = jnp.imag(far_box).astype(jnp.bfloat16).reshape(K, R * BOXES)
    far_re = contract_first(farb_re, decode[0]) - contract_first(farb_im, decode[1])
    far_im = contract_first(farb_im, decode[0]) + contract_first(farb_re, decode[1])
    far_part = jnp.stack([far_re.reshape(R, BOXES, P_SIZE), far_im.reshape(R, BOXES, P_SIZE)], axis=0).transpose(2, 0, 1, 3)

    def near_box(packed):
        blocks, source_ids, marks = packed
        picked = sources[source_ids].astype(jnp.float32) * marks.astype(jnp.float32)[:, None, None, None]
        blocks = blocks.astype(jnp.float32)
        near_re = jnp.einsum("spq,srq->rp", blocks[:, 0], picked[:, 0]) - jnp.einsum("spq,srq->rp", blocks[:, 1], picked[:, 1])
        near_im = jnp.einsum("spq,srq->rp", blocks[:, 0], picked[:, 1]) + jnp.einsum("spq,srq->rp", blocks[:, 1], picked[:, 0])
        return jnp.stack([near_re, near_im], axis=0)

    near_part = lax.map(near_box, (near_blocks, near_list, near_mask))
    return far_part + near_part
```

```python
import functools
import math

import jax
import jax.numpy as jnp
import numpy as np
from jax import lax
from jax.experimental import pallas as pl
from jax.experimental.pallas import tpu as pltpu
from jax.sharding import PartitionSpec as P

GY = 8
GZ = 4
LANES = 128

F32 = jnp.float32
BF16 = jnp.bfloat16


def dot_nt(left, right):
    return lax.dot_general(left, right, (((1,), (1,)), ((), ())), preferred_element_type=F32)


def dot_nn(left, right):
    return lax.dot_general(left, right, (((1,), (0,)), ((), ())), preferred_element_type=F32)


def split(value):
    high = value.astype(BF16)
    return high, (value - high.astype(F32)).astype(BF16)


def plane_table(points_y, points_z):
    freq = np.arange(4 * GY * GZ)
    turns = np.outer(freq // (2 * GZ), points_y) % (2 * GY) / (2 * GY)
    turns = turns + np.outer(freq % (2 * GZ), points_z) % (2 * GZ) / (2 * GZ)
    cosine, sine = np.cos(2.0 * math.pi * turns), np.sin(2.0 * math.pi * turns)
    table = np.block([[cosine, sine], [-sine, cosine]]).astype(np.float32)
    high = table.astype(BF16)
    return high, (table - high.astype(np.float32)).astype(BF16)


def part_rows(box, rhs):
    start = 2 * box * rhs
    return slice(start, start + rhs), slice(start + rhs, start + 2 * rhs)


def encode_kernel(rhs, group, src_ref, enc_ref, out_ref, coded_ref):
    src = src_ref[...]
    with_re = dot_nt(src, enc_ref[0])
    with_im = dot_nt(src, enc_ref[1])
    rows = src.shape[0] // rhs
    pieces = LANES // group
    for block in range(coded_ref.shape[0]):
        cols = slice(block * LANES, (block + 1) * LANES)
        for box in range(rows // 2):
            re, im = part_rows(box, rhs)
            coded_ref[block, re, :] = with_re[re, cols] - with_im[im, cols]
            coded_ref[block, im, :] = with_re[im, cols] + with_im[re, cols]
    for block in range(coded_ref.shape[0]):
        flat = coded_ref.at[block]
        for tile in range(rhs // pieces):
            parts = [flat[pl.ds(tile * pieces + n, rows, stride=rhs), :] for n in range(pieces)]
            for slot in range(pieces):
                lanes = slice(slot * group, (slot + 1) * group)
                out_ref[block * pieces + slot, :, tile * LANES : (tile + 1) * LANES] = jnp.concatenate(
                    [part[:, lanes] for part in parts], axis=1
                ).astype(BF16)


def table_kernel(grid_x, kern_ref, row_ref, col_ref, cell_hi, cell_lo, full_hi, full_lo, fwd_ref, inv_ref, spec_ref):
    plane = full_hi.shape[0] // 2
    cells = GY * GZ
    boxes = row_ref.shape[1]
    cell_row, cell_col = row_ref[...], col_ref[...]
    down = lax.broadcasted_iota(jnp.int32, (2 * cells, boxes), 0)
    part_row = lax.broadcasted_iota(jnp.int32, (2 * cells, boxes), 1) % 2
    across = lax.broadcasted_iota(jnp.int32, (boxes, 2 * cells), 1)
    part_col = lax.broadcasted_iota(jnp.int32, (boxes, 2 * cells), 0) % 2
    for x in range(grid_x):
        hit = (cell_row - x * cells + part_row * cells == down) & (cell_row // cells == x)
        place = jnp.where(hit, 1.0, 0.0).astype(BF16)
        fwd_ref[x, :, :boxes] = dot_nn(cell_hi[...], place).astype(BF16)
        fwd_ref[x, :, boxes:] = dot_nn(cell_lo[...], place).astype(BF16)
        hit = (cell_col - x * cells + part_col * cells == across) & (cell_col // cells == x)
        place = jnp.where(hit, 1.0 / plane, 0.0).astype(BF16)
        inv_ref[x, 0] = dot_nt(place, cell_hi[...]).astype(BF16)
        inv_ref[x, 1] = dot_nt(place, cell_lo[...]).astype(BF16)
    point = lax.broadcasted_iota(jnp.int32, (1, 2 * plane), 1) % plane
    off_y, off_z = point // (2 * GZ), point % (2 * GZ)
    close = ((off_y <= 1) | (off_y == 2 * GY - 1)) & ((off_z <= 1) | (off_z == 2 * GZ - 1))
    keep = jnp.where(close, 0.0, 1.0)
    repeat = LANES // kern_ref.shape[0]
    double_x = kern_ref.shape[2]
    for off in range(double_x):
        if off == grid_x:
            continue
        kept = jnp.concatenate([kern_ref[:, 0, off, :], kern_ref[:, 1, off, :]], axis=1)
        if off <= 1 or off == double_x - 1:
            kept = kept * keep
        high, low = split(kept)
        high = jnp.concatenate([high] * repeat, axis=0)
        low = jnp.concatenate([low] * repeat, axis=0)
        spec_ref[off] = dot_nt(full_hi[...], high) + dot_nt(full_hi[...], low) + dot_nt(full_lo[...], high)


def far_kernel(grid_x, coded_ref, fwd_ref, inv_ref, spec_ref, out_ref):
    owners, rows, width = coded_ref.shape
    plane = spec_ref.shape[1] // 2
    double_x = spec_ref.shape[0]
    step = min(2 * LANES, width)
    for start in range(0, width, step):
        cols = slice(start, start + step)
        coded = coded_ref[:, :, cols].reshape(owners * rows, step)
        coded = jnp.concatenate([coded, coded], axis=0)
        data = [dot_nn(fwd_ref[x], coded) for x in range(grid_x)]
        total = None
        for x in range(grid_x):
            tiles = []
            for tile in range(step // LANES):
                lanes = slice(tile * LANES, (tile + 1) * LANES)
                re = im = None
                for s in range(grid_x):
                    off = (x - s) % double_x
                    s_re, s_im = spec_ref[off, :plane], spec_ref[off, plane:]
                    d_re, d_im = data[s][:plane, lanes], data[s][plane:, lanes]
                    p_re = d_re * s_re - d_im * s_im
                    p_im = d_re * s_im + d_im * s_re
                    re = p_re if re is None else re + p_re
                    im = p_im if im is None else im + p_im
                tiles.append(jnp.concatenate([re, im], axis=0))
            high, low = split(jnp.concatenate(tiles, axis=1))
            term = dot_nn(inv_ref[x, 0], high) + dot_nn(inv_ref[x, 0], low) + dot_nn(inv_ref[x, 1], high)
            total = term if total is None else total + term
        out_ref[:, :, cols] = total.astype(BF16).reshape(owners, rows, step)


def near_kernel(share, list_ref, mask_ref, where_ref, mine_ref, theirs_ref, blocks_ref, out_ref, src, blk, acc, src_sem, blk_sem):
    boxes, slots = blocks_ref.shape[0], blocks_ref.shape[1]
    count = boxes * slots
    unknowns = blocks_ref.shape[4]
    me, side = where_ref[0], where_ref[1]
    own = pltpu.make_async_copy(mine_ref, src.at[side], src_sem.at[0])
    other = pltpu.make_async_copy(theirs_ref, src.at[1 - side], src_sem.at[1])
    own.start()
    other.start()

    def block_copy(box, slot):
        n = box * slots + slot
        return pltpu.make_async_copy(blocks_ref.at[box, slot], blk.at[n], blk_sem.at[n])

    for box in range(boxes):

        @pl.loop(0, slots)
        def _(slot):
            @pl.when(mask_ref[box * slots + slot] != 0)
            def _():
                block_copy(box, slot).start()

    own.wait()
    other.wait()
    half = src.shape[3] // 2
    for box in range(boxes):
        acc[...] = jnp.zeros_like(acc)

        @pl.loop(0, slots)
        def _(slot):
            n = box * slots + slot

            @pl.when(mask_ref[n] != 0)
            def _():
                block_copy(box, slot).wait()
                source = list_ref[n]
                owner, place = source // boxes, source % boxes
                vector = src[place // share, owner ^ me, place % share]
                acc[...] += jnp.concatenate([dot_nt(vector, blk[n, 0]), dot_nt(vector, blk[n, 1])], axis=1)

        re, im = slice(0, half), slice(half, 2 * half)
        with_re, with_im = acc[:, :unknowns], acc[:, unknowns:]
        base = box * 2 * half
        out_ref[base : base + half, :] = with_re[re] - with_im[im]
        out_ref[base + half : base + 2 * half, :] = with_re[im] + with_im[re]


def decode_kernel(rhs, group, where_ref, far_ref, dec_ref, near_ref, own_ref, other_ref, wide, total):
    owners, rows, width = far_ref.shape
    pieces = LANES // group
    for block in range(wide.shape[0]):
        flat = wide.at[block]
        for tile in range(width // LANES):
            cols = slice(tile * LANES, (tile + 1) * LANES)
            parts = [far_ref[block * pieces + slot, :, cols].astype(F32) for slot in range(pieces)]
            for n in range(pieces):
                lanes = slice(n * group, (n + 1) * group)
                flat[pl.ds(tile * pieces + n, rows, stride=rhs), :] = jnp.concatenate(
                    [part[:, lanes] for part in parts], axis=1
                )
    fields = jnp.concatenate([wide[block].astype(BF16) for block in range(wide.shape[0])], axis=1)
    with_re = dot_nn(fields, dec_ref[0])
    with_im = dot_nn(fields, dec_ref[1])
    for box in range(rows // 2):
        re, im = part_rows(box, rhs)
        total[re, :] = near_ref[re, :] + (with_re[re] - with_im[im])
        total[im, :] = near_ref[im, :] + (with_re[im] + with_im[re])
    half = total.shape[1] // 2
    first = where_ref[1] == 0
    left, right = total[:, :half], total[:, half:]
    own_ref[...] = jnp.where(first, left, right)
    other_ref[...] = jnp.where(first, right, left)


def gather_shares(share):
    size = lax.axis_size("box")
    held = share[None]
    low = size
    while low > 1:
        fan = 4 if low % 4 == 0 else 2
        low //= fan
        moved = [held]
        for delta in range(1, fan):
            moved.append(lax.ppermute(held, "box", [(i, i ^ (delta * low)) for i in range(size)]))
        held = jnp.stack(moved, axis=1).reshape((-1,) + share.shape)
    return held


def vmem():
    return pl.BlockSpec(memory_space=pltpu.VMEM)


def smem():
    return pl.BlockSpec(memory_space=pltpu.SMEM)


def anywhere():
    return pl.BlockSpec(memory_space=pl.ANY)


def on_device(sources, encode, kernel, decode, near_blocks, near_list, near_mask, box_cell):
    owners, sides = lax.axis_size("box"), lax.axis_size("dir")
    per_box, parts, rhs, unknowns = sources.shape
    group_dirs, _, double_x, plane = kernel.shape
    side_dirs = encode.shape[1]
    grid_x = double_x // 2
    rows = per_box * parts
    width = rhs * group_dirs
    boxes = box_cell.shape[0]
    me, side = lax.axis_index("box"), lax.axis_index("dir")
    where = jnp.stack([me, side]).astype(jnp.int32)

    share = per_box // sides
    own_share = lax.dynamic_slice_in_dim(sources, side * share, share, 0)
    mine = gather_shares(own_share.reshape(share, parts * rhs, unknowns))
    theirs = lax.ppermute(mine, "dir", [(i, 1 - i) for i in range(sides)])

    coded = pl.pallas_call(
        functools.partial(encode_kernel, rhs, group_dirs),
        out_shape=jax.ShapeDtypeStruct((owners, rows, width), BF16),
        in_specs=[vmem(), vmem()],
        out_specs=vmem(),
        scratch_shapes=[pltpu.VMEM((side_dirs // LANES, rows * rhs, LANES), F32)],
        name="encode",
    )(sources.reshape(rows * rhs, unknowns), encode)
    arrived = lax.all_to_all(coded, "box", split_axis=0, concat_axis=0, tiled=True)

    cell = np.arange(GY * GZ)
    cell_hi, cell_lo = plane_table(cell // GZ, cell % GZ)
    point = np.arange(plane)
    full_hi, full_lo = plane_table(point // (2 * GZ), point % (2 * GZ))
    cells = jnp.repeat(box_cell, parts)
    forward, inverse, spectrum = pl.pallas_call(
        functools.partial(table_kernel, grid_x),
        out_shape=(
            jax.ShapeDtypeStruct((grid_x, 2 * plane, 2 * parts * boxes), BF16),
            jax.ShapeDtypeStruct((grid_x, 2, parts * boxes, 2 * plane), BF16),
            jax.ShapeDtypeStruct((double_x, 2 * plane, LANES), F32),
        ),
        in_specs=[vmem()] * 7,
        out_specs=(vmem(),) * 3,
        name="tables",
    )(kernel, cells[None, :], cells[:, None], cell_hi, cell_lo, full_hi, full_lo)

    far = pl.pallas_call(
        functools.partial(far_kernel, grid_x),
        out_shape=jax.ShapeDtypeStruct((owners, rows, width), BF16),
        in_specs=[vmem()] * 4,
        out_specs=vmem(),
        name="far",
    )(arrived, forward, inverse, spectrum)
    returned = lax.all_to_all(far, "box", split_axis=0, concat_axis=0, tiled=True)

    slots = near_list.shape[1]
    near = pl.pallas_call(
        functools.partial(near_kernel, share),
        out_shape=jax.ShapeDtypeStruct((rows * rhs, unknowns), F32),
        in_specs=[smem(), smem(), smem(), anywhere(), anywhere(), anywhere()],
        out_specs=vmem(),
        scratch_shapes=[
            pltpu.VMEM((sides, owners, share, parts * rhs, unknowns), BF16),
            pltpu.VMEM((per_box * slots, parts, unknowns, unknowns), BF16),
            pltpu.VMEM((parts * rhs, parts * unknowns), F32),
            pltpu.SemaphoreType.DMA((2,)),
            pltpu.SemaphoreType.DMA((per_box * slots,)),
        ],
        name="near",
    )(near_list.reshape(-1), near_mask.reshape(-1), where, mine, theirs, near_blocks)

    half = unknowns // sides
    own, other = pl.pallas_call(
        functools.partial(decode_kernel, rhs, group_dirs),
        out_shape=(jax.ShapeDtypeStruct((rows * rhs, half), F32),) * 2,
        in_specs=[smem(), vmem(), vmem(), vmem()],
        out_specs=(vmem(),) * 2,
        scratch_shapes=[
            pltpu.VMEM((side_dirs // LANES, rows * rhs, LANES), F32),
            pltpu.VMEM((rows * rhs, unknowns), F32),
        ],
        name="decode",
    )(where, returned, decode, near)
    swapped = lax.ppermute(other, "dir", [(i, 1 - i) for i in range(sides)])
    return (own + swapped).reshape(per_box, parts, rhs, half)


def solution(mesh):
    in_specs = (
        P("box", None, None, None),
        P(None, "dir", None),
        P(("dir", "box"), None, None, None),
        P(None, "dir", None),
        P("box", "dir", None, None, None),
        P("box", "dir"),
        P("box", "dir"),
        P(),
    )
    out_specs = P("box", None, None, "dir")
    return jax.shard_map(
        on_device, mesh=mesh, in_specs=in_specs, out_specs=out_specs, check_vma=False
    )
```

```python
import functools
import math

import jax
import jax.numpy as jnp
import numpy as np
from jax import lax
from jax.experimental import pallas as pl
from jax.experimental.pallas import tpu as pltpu
from jax.sharding import PartitionSpec as P


GY = 8
GZ = 4
LANES = 128

F32 = jnp.float32
BF16 = jnp.bfloat16


def dot_nt(left, right):
    return lax.dot_general(left, right, (((1,), (1,)), ((), ())), preferred_element_type=F32)


def dot_nn(left, right):
    return lax.dot_general(left, right, (((1,), (0,)), ((), ())), preferred_element_type=F32)


def split(value):
    high = value.astype(BF16)
    return high, (value - high.astype(F32)).astype(BF16)


def plane_table(points_y, points_z):
    freq = np.arange(4 * GY * GZ)
    turns = np.outer(freq // (2 * GZ), points_y) % (2 * GY) / (2 * GY)
    turns = turns + np.outer(freq % (2 * GZ), points_z) % (2 * GZ) / (2 * GZ)
    cosine, sine = np.cos(2.0 * math.pi * turns), np.sin(2.0 * math.pi * turns)
    table = np.block([[cosine, sine], [-sine, cosine]]).astype(np.float32)
    high = table.astype(BF16)
    return high, (table - high.astype(np.float32)).astype(BF16)


def part_rows(box, rhs):
    start = 2 * box * rhs
    return slice(start, start + rhs), slice(start + rhs, start + 2 * rhs)


def encode_kernel(rhs, group, src_hbm, enc_hbm, out_ref, share_ref, src_ref, enc_ref, coded_ref, sem):
    copies = [
        pltpu.make_async_copy(src_hbm, src_ref, sem.at[0]),
        pltpu.make_async_copy(enc_hbm.at[0], enc_ref.at[0], sem.at[1]),
        pltpu.make_async_copy(enc_hbm.at[1], enc_ref.at[1], sem.at[2]),
    ]
    for copy in copies:
        copy.start()
    copies[0].wait()
    src = src_ref[...]
    part = src.shape[0] // lax.axis_size("dir")
    share_ref[...] = src_ref[pl.ds(pl.multiple_of(lax.axis_index("dir") * part, part), part), :]
    copies[1].wait()
    with_re = dot_nt(src, enc_ref[0])
    copies[2].wait()
    with_im = dot_nt(src, enc_ref[1])
    rows = src.shape[0] // rhs
    pieces = LANES // group
    for block in range(coded_ref.shape[0]):
        cols = slice(block * LANES, (block + 1) * LANES)
        for box in range(rows // 2):
            re, im = part_rows(box, rhs)
            coded_ref[block, re, :] = with_re[re, cols] - with_im[im, cols]
            coded_ref[block, im, :] = with_re[im, cols] + with_im[re, cols]
    for block in range(coded_ref.shape[0]):
        flat = coded_ref.at[block]
        for tile in range(rhs // pieces):
            parts = [flat[pl.ds(tile * pieces + n, rows, stride=rhs), :] for n in range(pieces)]
            for slot in range(pieces):
                lanes = slice(slot * group, (slot + 1) * group)
                out_ref[block * pieces + slot, :, tile * LANES : (tile + 1) * LANES] = jnp.concatenate(
                    [part[:, lanes] for part in parts], axis=1
                ).astype(BF16)


def table_kernel(grid_x, parts, box_hbm, kern_hbm, cell_hbm, full_hbm, fwd_ref, inv_ref, spec_ref, box_ref, kern_ref, cell_ref, full_ref, sem):
    copies = [
        pltpu.make_async_copy(box_hbm, box_ref, sem.at[0]),
        pltpu.make_async_copy(cell_hbm, cell_ref, sem.at[1]),
        pltpu.make_async_copy(kern_hbm, kern_ref, sem.at[2]),
        pltpu.make_async_copy(full_hbm, full_ref, sem.at[3]),
    ]
    for copy in copies:
        copy.start()
    full_hi, full_lo = full_ref.at[0], full_ref.at[1]
    cell_hi, cell_lo = cell_ref.at[0], cell_ref.at[1]
    plane = full_hi.shape[0] // 2
    cells = GY * GZ
    count = box_ref.shape[1]
    boxes = count * parts
    copies[0].wait()
    copies[1].wait()
    same = lax.broadcasted_iota(jnp.int32, (boxes, count), 0) // parts == lax.broadcasted_iota(jnp.int32, (boxes, count), 1)
    cell_col = jnp.sum(jnp.where(same, box_ref[...], 0), axis=1, keepdims=True)
    spread = jnp.where(same, 1.0, 0.0).astype(BF16)
    cell_row = dot_nt(jnp.broadcast_to(box_ref[...], (8, count)).astype(BF16), spread)[:1].astype(jnp.int32)
    down = lax.broadcasted_iota(jnp.int32, (2 * cells, boxes), 0)
    part_row = lax.broadcasted_iota(jnp.int32, (2 * cells, boxes), 1) % 2
    across = lax.broadcasted_iota(jnp.int32, (boxes, 2 * cells), 1)
    part_col = lax.broadcasted_iota(jnp.int32, (boxes, 2 * cells), 0) % 2
    for x in range(grid_x):
        hit = (cell_row - x * cells + part_row * cells == down) & (cell_row // cells == x)
        place = jnp.where(hit, 1.0, 0.0).astype(BF16)
        fwd_ref[x, :, :boxes] = dot_nn(cell_hi[...], place).astype(BF16)
        fwd_ref[x, :, boxes:] = dot_nn(cell_lo[...], place).astype(BF16)
        hit = (cell_col - x * cells + part_col * cells == across) & (cell_col // cells == x)
        place = jnp.where(hit, 1.0 / plane, 0.0).astype(BF16)
        inv_ref[x, 0] = dot_nt(place, cell_hi[...]).astype(BF16)
        inv_ref[x, 1] = dot_nt(place, cell_lo[...]).astype(BF16)
    point = lax.broadcasted_iota(jnp.int32, (1, 2 * plane), 1) % plane
    off_y, off_z = point // (2 * GZ), point % (2 * GZ)
    close = ((off_y <= 1) | (off_y == 2 * GY - 1)) & ((off_z <= 1) | (off_z == 2 * GZ - 1))
    keep = jnp.where(close, 0.0, 1.0)
    copies[2].wait()
    copies[3].wait()
    repeat = LANES // kern_ref.shape[0]
    double_x = kern_ref.shape[2]
    for off in range(double_x):
        if off == grid_x:
            continue
        kept = jnp.concatenate([kern_ref[:, 0, off, :], kern_ref[:, 1, off, :]], axis=1)
        if off <= 1 or off == double_x - 1:
            kept = kept * keep
        high, low = split(kept)
        high = jnp.concatenate([high] * repeat, axis=0)
        low = jnp.concatenate([low] * repeat, axis=0)
        spec_ref[off] = dot_nt(full_hi[...], high) + dot_nt(full_hi[...], low) + dot_nt(full_lo[...], high)


def far_kernel(grid_x, coded_ref, fwd_ref, inv_ref, spec_ref, out_ref):
    owners, rows, width = coded_ref.shape
    plane = spec_ref.shape[1] // 2
    double_x = spec_ref.shape[0]
    step = min(2 * LANES, width)
    for start in range(0, width, step):
        cols = slice(start, start + step)
        coded = coded_ref[:, :, cols].reshape(owners * rows, step)
        coded = jnp.concatenate([coded, coded], axis=0)
        data = [dot_nn(fwd_ref[x], coded) for x in range(grid_x)]
        total = None
        for x in range(grid_x):
            tiles = []
            for tile in range(step // LANES):
                lanes = slice(tile * LANES, (tile + 1) * LANES)
                re = im = None
                for s in range(grid_x):
                    off = (x - s) % double_x
                    s_re, s_im = spec_ref[off, :plane], spec_ref[off, plane:]
                    d_re, d_im = data[s][:plane, lanes], data[s][plane:, lanes]
                    p_re = d_re * s_re - d_im * s_im
                    p_im = d_re * s_im + d_im * s_re
                    re = p_re if re is None else re + p_re
                    im = p_im if im is None else im + p_im
                tiles.append(jnp.concatenate([re, im], axis=0))
            high, low = split(jnp.concatenate(tiles, axis=1))
            term = dot_nn(inv_ref[x, 0], high) + dot_nn(inv_ref[x, 0], low) + dot_nn(inv_ref[x, 1], high)
            total = term if total is None else total + term
        out_ref[:, :, cols] = total.astype(BF16).reshape(owners, rows, step)


def near_kernel(share, mine, list_ref, mask_ref, src_ref, blocks_ref, base_ref, out_ref, blk, acc, sem):
    boxes, slots = blocks_ref.shape[0], blocks_ref.shape[1]
    unknowns = blocks_ref.shape[4]
    me, side = lax.axis_index("box"), lax.axis_index("dir")
    wanted = side if mine else 1 - side

    def used(box, slot):
        return (mask_ref[box, slot] != 0) & (list_ref[box, slot] % boxes // share == wanted)

    def block_copy(box, slot):
        n = box * slots + slot
        return pltpu.make_async_copy(blocks_ref.at[box, slot], blk.at[n], sem.at[n])

    for box in range(boxes):

        @pl.loop(0, slots)
        def _(slot):
            @pl.when(used(box, slot))
            def _():
                block_copy(box, slot).start()

    half = src_ref.shape[2] // 2
    for box in range(boxes):
        acc[...] = jnp.zeros_like(acc)

        @pl.loop(0, slots)
        def _(slot):
            @pl.when(used(box, slot))
            def _():
                block_copy(box, slot).wait()
                n = box * slots + slot
                source = list_ref[box, slot]
                vector = src_ref[(source // boxes) ^ me, source % share]
                acc[...] += jnp.concatenate([dot_nt(vector, blk[n, 0]), dot_nt(vector, blk[n, 1])], axis=1)

        re, im = slice(0, half), slice(half, 2 * half)
        with_re, with_im = acc[:, :unknowns], acc[:, unknowns:]
        near_re = with_re[re] - with_im[im]
        near_im = with_re[im] + with_im[re]
        rows_re, rows_im = part_rows(box, half)
        if not mine:
            near_re = near_re + base_ref[rows_re, :]
            near_im = near_im + base_ref[rows_im, :]
        out_ref[rows_re, :] = near_re
        out_ref[rows_im, :] = near_im


def decode_kernel(rhs, group, far_ref, dec_ref, near_ref, own_ref, other_ref, wide, total):
    _, rows, width = far_ref.shape
    pieces = LANES // group
    for block in range(wide.shape[0]):
        flat = wide.at[block]
        for tile in range(width // LANES):
            cols = slice(tile * LANES, (tile + 1) * LANES)
            parts = [far_ref[block * pieces + slot, :, cols].astype(F32) for slot in range(pieces)]
            for n in range(pieces):
                lanes = slice(n * group, (n + 1) * group)
                flat[pl.ds(tile * pieces + n, rows, stride=rhs), :] = jnp.concatenate(
                    [part[:, lanes] for part in parts], axis=1
                )
    fields = jnp.concatenate([wide[block].astype(BF16) for block in range(wide.shape[0])], axis=1)
    with_re = dot_nn(fields, dec_ref[0])
    with_im = dot_nn(fields, dec_ref[1])
    for box in range(rows // 2):
        re, im = part_rows(box, rhs)
        total[re, :] = near_ref[re, :] + (with_re[re] - with_im[im])
        total[im, :] = near_ref[im, :] + (with_re[im] + with_im[re])
    half = total.shape[1] // 2
    first = lax.axis_index("dir") == 0
    left, right = total[:, :half], total[:, half:]
    own_ref[...] = jnp.where(first, left, right)
    other_ref[...] = jnp.where(first, right, left)


def join_kernel(*refs):
    for n, ref in enumerate(refs[:-1]):
        refs[-1][:, n] = ref[...]


def join(pieces):
    shape = pieces[0].shape
    joined = pl.pallas_call(
        join_kernel,
        out_shape=pltpu.VMEM((shape[0], len(pieces)) + shape[1:], pieces[0].dtype),
        in_specs=[vmem()] * len(pieces),
        out_specs=vmem(),
        compiler_params=budget(4),
        name="join",
    )(*pieces)
    return joined.reshape((-1,) + shape[1:])


def gather_shares(share):
    size = lax.axis_size("box")
    held = share[None]
    low = size
    while low > 1:
        fan = 4 if low % 4 == 0 else 2
        low //= fan
        moved = [held]
        for delta in range(1, fan):
            moved.append(lax.ppermute(held, "box", [(i, i ^ (delta * low)) for i in range(size)]))
        held = join(moved)
    return held


def budget(mebibytes):
    return pltpu.CompilerParams(vmem_limit_bytes=mebibytes << 20)


def stay(array):
    return pltpu.with_memory_space_constraint(array, pltpu.HBM)


def vmem():
    return pl.BlockSpec(memory_space=pltpu.VMEM)


def smem():
    return pl.BlockSpec(memory_space=pltpu.SMEM)


def hbm():
    return pl.BlockSpec(memory_space=pltpu.HBM)


def whole_product(sources, encode, kernel, decode, near_blocks, near_list, near_mask, box_cell):
    owners, sides = lax.axis_size("box"), lax.axis_size("dir")
    per_box, parts, rhs, unknowns = sources.shape
    group_dirs, _, double_x, plane = kernel.shape
    side_dirs = encode.shape[1]
    grid_x = double_x // 2
    rows = per_box * parts
    width = rhs * group_dirs
    boxes = box_cell.shape[0]

    share = per_box // sides
    coded, own_share = pl.pallas_call(
        functools.partial(encode_kernel, rhs, group_dirs),
        out_shape=(
            pltpu.VMEM((owners, rows, width), BF16),
            pltpu.VMEM((share * parts * rhs, unknowns), BF16),
        ),
        in_specs=[hbm(), hbm()],
        out_specs=(vmem(),) * 2,
        scratch_shapes=[
            pltpu.VMEM((rows * rhs, unknowns), BF16),
            pltpu.VMEM(encode.shape, BF16),
            pltpu.VMEM((side_dirs // LANES, rows * rhs, LANES), F32),
            pltpu.SemaphoreType.DMA((3,)),
        ],
        compiler_params=budget(8),
        name="encode",
    )(stay(sources.reshape(rows * rhs, unknowns)), stay(encode))
    arrived = lax.all_to_all(coded, "box", split_axis=0, concat_axis=0, tiled=True)
    mine = gather_shares(own_share.reshape(share, parts * rhs, unknowns))
    theirs = lax.ppermute(mine, "dir", [(i, 1 - i) for i in range(sides)])

    cell = np.arange(GY * GZ)
    cell_hi, cell_lo = plane_table(cell // GZ, cell % GZ)
    point = np.arange(plane)
    full_hi, full_lo = plane_table(point // (2 * GZ), point % (2 * GZ))
    constants = (np.stack([cell_hi, cell_lo]), np.stack([full_hi, full_lo]))
    forward, inverse, spectrum = pl.pallas_call(
        functools.partial(table_kernel, grid_x, parts),
        out_shape=(
            pltpu.VMEM((grid_x, 2 * plane, 2 * parts * boxes), BF16),
            pltpu.VMEM((grid_x, 2, parts * boxes, 2 * plane), BF16),
            pltpu.VMEM((double_x, 2 * plane, LANES), F32),
        ),
        in_specs=[hbm()] * 4,
        out_specs=(vmem(),) * 3,
        scratch_shapes=[
            pltpu.VMEM((1, boxes), jnp.int32),
            pltpu.VMEM(kernel.shape, F32),
            pltpu.VMEM(constants[0].shape, BF16),
            pltpu.VMEM(constants[1].shape, BF16),
            pltpu.SemaphoreType.DMA((4,)),
        ],
        compiler_params=budget(24),
        name="tables",
    )(stay(box_cell[None, :]), stay(kernel), *[stay(jnp.asarray(table)) for table in constants])

    far = pl.pallas_call(
        functools.partial(far_kernel, grid_x),
        out_shape=pltpu.VMEM((owners, rows, width), BF16),
        in_specs=[vmem()] * 4,
        out_specs=vmem(),
        compiler_params=budget(8),
        name="far",
    )(arrived, forward, inverse, spectrum)
    returned = lax.all_to_all(far, "box", split_axis=0, concat_axis=0, tiled=True)


    slots = near_list.shape[1]

    def near(is_mine, vectors, base):
        return pl.pallas_call(
            functools.partial(near_kernel, share, is_mine),
            out_shape=pltpu.VMEM((rows * rhs, unknowns), F32),
            in_specs=[smem(), smem(), vmem(), hbm(), vmem()],
            out_specs=vmem(),
            scratch_shapes=[
                pltpu.VMEM((per_box * slots, parts, unknowns, unknowns), BF16),
                pltpu.VMEM((parts * rhs, parts * unknowns), F32),
                pltpu.SemaphoreType.DMA((per_box * slots,)),
            ],
            compiler_params=budget(20),
            name="near_mine" if is_mine else "near_theirs",
        )(stay(near_list), stay(near_mask), vectors, stay(near_blocks), base)

    near_part = near(True, mine, own_share)
    near_part = near(False, theirs, near_part)

    half = unknowns // sides
    own, other = pl.pallas_call(
        functools.partial(decode_kernel, rhs, group_dirs),
        out_shape=(pltpu.VMEM((rows * rhs, half), F32),) * 2,
        in_specs=[vmem(), vmem(), vmem()],
        out_specs=(vmem(),) * 2,
        scratch_shapes=[
            pltpu.VMEM((side_dirs // LANES, rows * rhs, LANES), F32),
            pltpu.VMEM((rows * rhs, unknowns), F32),
        ],
        compiler_params=budget(8),
        name="decode",
    )(returned, decode, near_part)
    swapped = lax.ppermute(other, "dir", [(i, 1 - i) for i in range(sides)])
    return (own + swapped).reshape(per_box, parts, rhs, half)


def solution(mesh):
    in_specs = (
        P("box", None, None, None),
        P(None, "dir", None),
        P(("dir", "box"), None, None, None),
        P(None, "dir", None),
        P("box", "dir", None, None, None),
        P("box", "dir"),
        P("box", "dir"),
        P(),
    )
    out_specs = P("box", None, None, "dir")
    return jax.shard_map(whole_product, mesh=mesh, in_specs=in_specs, out_specs=out_specs, check_vma=False)
```

```python
import functools
import math

import jax
import jax.numpy as jnp
import numpy as np
from jax import lax
from jax.experimental import pallas as pl
from jax.experimental.pallas import tpu as pltpu
from jax.sharding import PartitionSpec as P


GY = 8
GZ = 4
LANES = 128

F32 = jnp.float32
BF16 = jnp.bfloat16


def dot_nt(left, right):
    return lax.dot_general(left, right, (((1,), (1,)), ((), ())), preferred_element_type=F32)


def dot_nn(left, right):
    return lax.dot_general(left, right, (((1,), (0,)), ((), ())), preferred_element_type=F32)


def split(value):
    high = value.astype(BF16)
    return high, (value - high.astype(F32)).astype(BF16)


def plane_table(points_y, points_z):
    freq = np.arange(4 * GY * GZ)
    turns = np.outer(freq // (2 * GZ), points_y) % (2 * GY) / (2 * GY)
    turns = turns + np.outer(freq % (2 * GZ), points_z) % (2 * GZ) / (2 * GZ)
    cosine, sine = np.cos(2.0 * math.pi * turns), np.sin(2.0 * math.pi * turns)
    table = np.block([[cosine, sine], [-sine, cosine]]).astype(np.float32)
    high = table.astype(BF16)
    return high, (table - high.astype(np.float32)).astype(BF16)


def part_rows(box, rhs):
    start = 2 * box * rhs
    return slice(start, start + rhs), slice(start + rhs, start + 2 * rhs)


def encode_kernel(rhs, group, src_hbm, enc_hbm, out_ref, share_ref, src_ref, enc_ref, coded_ref, sem):
    copies = [
        pltpu.make_async_copy(src_hbm, src_ref, sem.at[0]),
        pltpu.make_async_copy(enc_hbm.at[0], enc_ref.at[0], sem.at[1]),
        pltpu.make_async_copy(enc_hbm.at[1], enc_ref.at[1], sem.at[2]),
    ]
    for copy in copies:
        copy.start()
    copies[0].wait()
    src = src_ref[...]
    part = src.shape[0] // lax.axis_size("dir")
    share_ref[...] = src_ref[pl.ds(pl.multiple_of(lax.axis_index("dir") * part, part), part), :]
    copies[1].wait()
    with_re = dot_nt(src, enc_ref[0])
    copies[2].wait()
    with_im = dot_nt(src, enc_ref[1])
    rows = src.shape[0] // rhs
    pieces = LANES // group
    for block in range(coded_ref.shape[0]):
        cols = slice(block * LANES, (block + 1) * LANES)
        for box in range(rows // 2):
            re, im = part_rows(box, rhs)
            coded_ref[block, re, :] = with_re[re, cols] - with_im[im, cols]
            coded_ref[block, im, :] = with_re[im, cols] + with_im[re, cols]
    for block in range(coded_ref.shape[0]):
        flat = coded_ref.at[block]
        for tile in range(rhs // pieces):
            parts = [flat[pl.ds(tile * pieces + n, rows, stride=rhs), :] for n in range(pieces)]
            for slot in range(pieces):
                lanes = slice(slot * group, (slot + 1) * group)
                out_ref[block * pieces + slot, :, tile * LANES : (tile + 1) * LANES] = jnp.concatenate(
                    [part[:, lanes] for part in parts], axis=1
                ).astype(BF16)


def table_kernel(
    grid_x, parts, share, list_ref, mask_ref, box_hbm, kern_hbm, cell_hbm, full_hbm,
    fwd_ref, inv_ref, spec_ref, order_ref, box_ref, kern_ref, cell_ref, full_ref, sem,
):
    copies = [
        pltpu.make_async_copy(box_hbm, box_ref, sem.at[0]),
        pltpu.make_async_copy(cell_hbm, cell_ref, sem.at[1]),
        pltpu.make_async_copy(kern_hbm, kern_ref, sem.at[2]),
        pltpu.make_async_copy(full_hbm, full_ref, sem.at[3]),
    ]
    for copy in copies:
        copy.start()
    list_slots(share, list_ref, mask_ref, order_ref)
    full_hi, full_lo = full_ref.at[0], full_ref.at[1]
    cell_hi, cell_lo = cell_ref.at[0], cell_ref.at[1]
    plane = full_hi.shape[0] // 2
    cells = GY * GZ
    count = box_ref.shape[1]
    boxes = count * parts
    copies[0].wait()
    copies[1].wait()
    same = lax.broadcasted_iota(jnp.int32, (boxes, count), 0) // parts == lax.broadcasted_iota(jnp.int32, (boxes, count), 1)
    cell_col = jnp.sum(jnp.where(same, box_ref[...], 0), axis=1, keepdims=True)
    spread = jnp.where(same, 1.0, 0.0).astype(BF16)
    cell_row = dot_nt(jnp.broadcast_to(box_ref[...], (8, count)).astype(BF16), spread)[:1].astype(jnp.int32)
    down = lax.broadcasted_iota(jnp.int32, (2 * cells, boxes), 0)
    part_row = lax.broadcasted_iota(jnp.int32, (2 * cells, boxes), 1) % 2
    across = lax.broadcasted_iota(jnp.int32, (boxes, 2 * cells), 1)
    part_col = lax.broadcasted_iota(jnp.int32, (boxes, 2 * cells), 0) % 2
    for x in range(grid_x):
        hit = (cell_row - x * cells + part_row * cells == down) & (cell_row // cells == x)
        place = jnp.where(hit, 1.0, 0.0).astype(BF16)
        fwd_ref[x, :, :boxes] = dot_nn(cell_hi[...], place).astype(BF16)
        fwd_ref[x, :, boxes:] = dot_nn(cell_lo[...], place).astype(BF16)
        hit = (cell_col - x * cells + part_col * cells == across) & (cell_col // cells == x)
        place = jnp.where(hit, 1.0 / plane, 0.0).astype(BF16)
        inv_ref[x, 0] = dot_nt(place, cell_hi[...]).astype(BF16)
        inv_ref[x, 1] = dot_nt(place, cell_lo[...]).astype(BF16)
    point = lax.broadcasted_iota(jnp.int32, (1, 2 * plane), 1) % plane
    off_y, off_z = point // (2 * GZ), point % (2 * GZ)
    close = ((off_y <= 1) | (off_y == 2 * GY - 1)) & ((off_z <= 1) | (off_z == 2 * GZ - 1))
    keep = jnp.where(close, 0.0, 1.0)
    copies[2].wait()
    copies[3].wait()
    repeat = LANES // kern_ref.shape[0]
    double_x = kern_ref.shape[2]
    for off in range(double_x):
        if off == grid_x:
            continue
        kept = jnp.concatenate([kern_ref[:, 0, off, :], kern_ref[:, 1, off, :]], axis=1)
        if off <= 1 or off == double_x - 1:
            kept = kept * keep
        high, low = split(kept)
        high = jnp.concatenate([high] * repeat, axis=0)
        low = jnp.concatenate([low] * repeat, axis=0)
        spec_ref[off] = dot_nt(full_hi[...], high) + dot_nt(full_hi[...], low) + dot_nt(full_lo[...], high)


def far_kernel(grid_x, coded_ref, fwd_ref, inv_ref, spec_ref, out_ref):
    owners, rows, width = coded_ref.shape
    plane = spec_ref.shape[1] // 2
    double_x = spec_ref.shape[0]
    step = min(2 * LANES, width)
    for start in range(0, width, step):
        cols = slice(start, start + step)
        coded = coded_ref[:, :, cols].reshape(owners * rows, step)
        coded = jnp.concatenate([coded, coded], axis=0)
        data = [dot_nn(fwd_ref[x], coded) for x in range(grid_x)]
        total = None
        for x in range(grid_x):
            tiles = []
            for tile in range(step // LANES):
                lanes = slice(tile * LANES, (tile + 1) * LANES)
                re = im = None
                for s in range(grid_x):
                    off = (x - s) % double_x
                    s_re, s_im = spec_ref[off, :plane], spec_ref[off, plane:]
                    d_re, d_im = data[s][:plane, lanes], data[s][plane:, lanes]
                    p_re = d_re * s_re - d_im * s_im
                    p_im = d_re * s_im + d_im * s_re
                    re = p_re if re is None else re + p_re
                    im = p_im if im is None else im + p_im
                tiles.append(jnp.concatenate([re, im], axis=0))
            high, low = split(jnp.concatenate(tiles, axis=1))
            term = dot_nn(inv_ref[x, 0], high) + dot_nn(inv_ref[x, 0], low) + dot_nn(inv_ref[x, 1], high)
            total = term if total is None else total + term
        out_ref[:, :, cols] = total.astype(BF16).reshape(owners, rows, step)


def list_slots(share, list_ref, mask_ref, order_ref):
    boxes, slots = list_ref.shape
    count = boxes * slots
    me, side = lax.axis_index("box"), lax.axis_index("dir")
    owners = lax.axis_size("box")
    for box in range(boxes):

        def visit(slot, filled):
            valid = mask_ref[box, slot] != 0

            @pl.when(valid)
            def _():
                source = list_ref[box, slot]
                owner, place = lax.div(source, boxes), lax.rem(source, boxes)
                from_other = (lax.div(place, share) != side).astype(jnp.int32)
                entry = (from_other * owners + (owner ^ me)) * share + lax.rem(place, share)
                order_ref[box * slots + filled] = entry
                order_ref[count + box * slots + filled] = box * slots + slot

            return filled + valid.astype(jnp.int32)

        filled = lax.fori_loop(0, slots, visit, jnp.int32(0))
        order_ref[2 * count + box] = filled

        @pl.loop(filled, slots)
        def _(rank):
            order_ref[box * slots + rank] = 0
            order_ref[count + box * slots + rank] = count


def fetch_kernel(mask_ref, blocks_hbm, blk_ref, sem):
    boxes, slots = blocks_hbm.shape[0], blocks_hbm.shape[1]
    count = boxes * slots

    def visit(fn):
        for box in range(boxes):
            for slot in range(slots):

                @pl.when(mask_ref[box, slot] != 0)
                def _():
                    fn(pltpu.make_async_copy(blocks_hbm.at[box, slot], blk_ref.at[box * slots + slot], sem))

    visit(lambda copy: copy.start())
    blk_ref[count] = jnp.zeros(blk_ref.shape[1:], BF16)
    visit(lambda copy: copy.wait())


def near_kernel(boxes, order_ref, mine_ref, theirs_ref, blk_ref, out_ref, src, acc):
    count = blk_ref.shape[0] - 1
    slots = count // boxes
    held = mine_ref.shape[0] * mine_ref.shape[1]
    src[:held] = mine_ref[...].reshape((held,) + mine_ref.shape[2:])
    src[held:] = theirs_ref[...].reshape((held,) + theirs_ref.shape[2:])

    def product(box, ranks):
        entries = [box * slots + rank for rank in ranks]
        vectors = jnp.concatenate([src[order_ref[n]] for n in entries], axis=1)
        places = [order_ref[count + n] for n in entries]
        return [
            dot_nt(vectors, jnp.concatenate([blk_ref[place, part] for place in places], axis=1)) for part in range(2)
        ]

    first = (slots + 1) // 2 + 1
    for box in range(boxes):
        acc[box, 0], acc[box, 1] = product(box, range(first))
    for box in range(boxes):

        @pl.when(order_ref[2 * count + box] > first)
        def _():
            more = product(box, range(first, slots))
            acc[box, 0] += more[0]
            acc[box, 1] += more[1]

    half = src.shape[1] // 2
    re, im = slice(0, half), slice(half, 2 * half)
    for box in range(boxes):
        rows_re, rows_im = part_rows(box, half)
        out_ref[rows_re, :] = acc[box, 0, re, :] - acc[box, 1, im, :]
        out_ref[rows_im, :] = acc[box, 0, im, :] + acc[box, 1, re, :]


def decode_kernel(rhs, group, far_ref, dec_ref, near_ref, own_ref, other_ref, wide, total):
    _, rows, width = far_ref.shape
    pieces = LANES // group
    for block in range(wide.shape[0]):
        flat = wide.at[block]
        for tile in range(width // LANES):
            cols = slice(tile * LANES, (tile + 1) * LANES)
            parts = [far_ref[block * pieces + slot, :, cols].astype(F32) for slot in range(pieces)]
            for n in range(pieces):
                lanes = slice(n * group, (n + 1) * group)
                flat[pl.ds(tile * pieces + n, rows, stride=rhs), :] = jnp.concatenate(
                    [part[:, lanes] for part in parts], axis=1
                )
    fields = jnp.concatenate([wide[block].astype(BF16) for block in range(wide.shape[0])], axis=1)
    with_re = dot_nn(fields, dec_ref[0])
    with_im = dot_nn(fields, dec_ref[1])
    for box in range(rows // 2):
        re, im = part_rows(box, rhs)
        total[re, :] = near_ref[re, :] + (with_re[re] - with_im[im])
        total[im, :] = near_ref[im, :] + (with_re[im] + with_im[re])
    half = total.shape[1] // 2
    first = lax.axis_index("dir") == 0
    left, right = total[:, :half], total[:, half:]
    own_ref[...] = jnp.where(first, left, right)
    other_ref[...] = jnp.where(first, right, left)


def join_kernel(*refs):
    for n, ref in enumerate(refs[:-1]):
        refs[-1][:, n] = ref[...]


def join(pieces):
    shape = pieces[0].shape
    joined = pl.pallas_call(
        join_kernel,
        out_shape=pltpu.VMEM((shape[0], len(pieces)) + shape[1:], pieces[0].dtype),
        in_specs=[vmem()] * len(pieces),
        out_specs=vmem(),
        compiler_params=budget(4),
        name="join",
    )(*pieces)
    return joined.reshape((-1,) + shape[1:])


def gather_shares(share):
    size = lax.axis_size("box")
    held = share[None]
    low = size
    while low > 1:
        fan = 4 if low % 4 == 0 else 2
        low //= fan
        moved = [held]
        for delta in range(1, fan):
            moved.append(lax.ppermute(held, "box", [(i, i ^ (delta * low)) for i in range(size)]))
        held = join(moved)
    return held


def budget(mebibytes):
    return pltpu.CompilerParams(vmem_limit_bytes=mebibytes << 20)


def stay(array):
    return pltpu.with_memory_space_constraint(array, pltpu.HBM)


def vmem():
    return pl.BlockSpec(memory_space=pltpu.VMEM)


def smem():
    return pl.BlockSpec(memory_space=pltpu.SMEM)


def hbm():
    return pl.BlockSpec(memory_space=pltpu.HBM)


def whole_product(sources, encode, kernel, decode, near_blocks, near_list, near_mask, box_cell):
    owners, sides = lax.axis_size("box"), lax.axis_size("dir")
    per_box, parts, rhs, unknowns = sources.shape
    group_dirs, _, double_x, plane = kernel.shape
    side_dirs = encode.shape[1]
    grid_x = double_x // 2
    rows = per_box * parts
    width = rhs * group_dirs
    boxes = box_cell.shape[0]

    share = per_box // sides
    coded, own_share = pl.pallas_call(
        functools.partial(encode_kernel, rhs, group_dirs),
        out_shape=(
            pltpu.VMEM((owners, rows, width), BF16),
            pltpu.VMEM((share * parts * rhs, unknowns), BF16),
        ),
        in_specs=[hbm(), hbm()],
        out_specs=(vmem(),) * 2,
        scratch_shapes=[
            pltpu.VMEM((rows * rhs, unknowns), BF16),
            pltpu.VMEM(encode.shape, BF16),
            pltpu.VMEM((side_dirs // LANES, rows * rhs, LANES), F32),
            pltpu.SemaphoreType.DMA((3,)),
        ],
        compiler_params=budget(8),
        name="encode",
    )(stay(sources.reshape(rows * rhs, unknowns)), stay(encode))
    arrived = lax.all_to_all(coded, "box", split_axis=0, concat_axis=0, tiled=True)
    mine = gather_shares(own_share.reshape(share, parts * rhs, unknowns))
    theirs = lax.ppermute(mine, "dir", [(i, 1 - i) for i in range(sides)])

    cell = np.arange(GY * GZ)
    cell_hi, cell_lo = plane_table(cell // GZ, cell % GZ)
    point = np.arange(plane)
    full_hi, full_lo = plane_table(point // (2 * GZ), point % (2 * GZ))
    constants = (np.stack([cell_hi, cell_lo]), np.stack([full_hi, full_lo]))
    count = per_box * near_list.shape[1]
    forward, inverse, spectrum, order = pl.pallas_call(
        functools.partial(table_kernel, grid_x, parts, share),
        out_shape=(
            pltpu.VMEM((grid_x, 2 * plane, 2 * parts * boxes), BF16),
            pltpu.VMEM((grid_x, 2, parts * boxes, 2 * plane), BF16),
            pltpu.VMEM((double_x, 2 * plane, LANES), F32),
            jax.ShapeDtypeStruct((2 * count + per_box,), jnp.int32),
        ),
        in_specs=[smem(), smem()] + [hbm()] * 4,
        out_specs=(vmem(), vmem(), vmem(), smem()),
        scratch_shapes=[
            pltpu.VMEM((1, boxes), jnp.int32),
            pltpu.VMEM(kernel.shape, F32),
            pltpu.VMEM(constants[0].shape, BF16),
            pltpu.VMEM(constants[1].shape, BF16),
            pltpu.SemaphoreType.DMA((4,)),
        ],
        compiler_params=budget(24),
        name="tables",
    )(stay(near_list), stay(near_mask), stay(box_cell[None, :]), stay(kernel), *[stay(jnp.asarray(table)) for table in constants])

    far = pl.pallas_call(
        functools.partial(far_kernel, grid_x),
        out_shape=pltpu.VMEM((owners, rows, width), BF16),
        in_specs=[vmem()] * 4,
        out_specs=vmem(),
        compiler_params=budget(8),
        name="far",
    )(arrived, forward, inverse, spectrum)
    returned = lax.all_to_all(far, "box", split_axis=0, concat_axis=0, tiled=True)


    blocks = pl.pallas_call(
        fetch_kernel,
        out_shape=pltpu.VMEM((count + 1,) + near_blocks.shape[2:], BF16),
        in_specs=[smem(), hbm()],
        out_specs=vmem(),
        scratch_shapes=[pltpu.SemaphoreType.DMA],
        compiler_params=budget(4),
        name="fetch",
    )(stay(near_mask), stay(near_blocks))
    near_part = pl.pallas_call(
        functools.partial(near_kernel, per_box),
        out_shape=pltpu.VMEM((rows * rhs, unknowns), F32),
        in_specs=[smem(), vmem(), vmem(), vmem()],
        out_specs=vmem(),
        scratch_shapes=[
            pltpu.VMEM((sides * owners * share, parts * rhs, unknowns), BF16),
            pltpu.VMEM((per_box, parts, parts * rhs, unknowns), F32),
        ],
        compiler_params=budget(12),
        name="near",
    )(order, mine, theirs, blocks)

    half = unknowns // sides
    own, other = pl.pallas_call(
        functools.partial(decode_kernel, rhs, group_dirs),
        out_shape=(pltpu.VMEM((rows * rhs, half), F32),) * 2,
        in_specs=[vmem(), vmem(), vmem()],
        out_specs=(vmem(),) * 2,
        scratch_shapes=[
            pltpu.VMEM((side_dirs // LANES, rows * rhs, LANES), F32),
            pltpu.VMEM((rows * rhs, unknowns), F32),
        ],
        compiler_params=budget(8),
        name="decode",
    )(returned, decode, near_part)
    swapped = lax.ppermute(other, "dir", [(i, 1 - i) for i in range(sides)])
    return (own + swapped).reshape(per_box, parts, rhs, half)


def solution(mesh):
    in_specs = (
        P("box", None, None, None),
        P(None, "dir", None),
        P(("dir", "box"), None, None, None),
        P(None, "dir", None),
        P("box", "dir", None, None, None),
        P("box", "dir"),
        P("box", "dir"),
        P(),
    )
    out_specs = P("box", None, None, "dir")
    return jax.shard_map(whole_product, mesh=mesh, in_specs=in_specs, out_specs=out_specs, check_vma=False)
```

```python
import functools
import math

import jax
import jax.numpy as jnp
import numpy as np
from jax import lax
from jax.experimental import pallas as pl
from jax.experimental.pallas import tpu as pltpu
from jax.sharding import PartitionSpec as P


GY = 8
GZ = 4
LANES = 128

F32 = jnp.float32
BF16 = jnp.bfloat16


def dot_nt(left, right):
    return lax.dot_general(left, right, (((1,), (1,)), ((), ())), preferred_element_type=F32)


def dot_nn(left, right):
    return lax.dot_general(left, right, (((1,), (0,)), ((), ())), preferred_element_type=F32)


def split(value):
    high = value.astype(BF16)
    return high, (value - high.astype(F32)).astype(BF16)


def plane_table(points_y, points_z):
    freq = np.arange(4 * GY * GZ)
    turns = np.outer(freq // (2 * GZ), points_y) % (2 * GY) / (2 * GY)
    turns = turns + np.outer(freq % (2 * GZ), points_z) % (2 * GZ) / (2 * GZ)
    cosine, sine = np.cos(2.0 * math.pi * turns), np.sin(2.0 * math.pi * turns)
    table = np.block([[cosine, sine], [-sine, cosine]]).astype(np.float32)
    high = table.astype(BF16)
    return high, (table - high.astype(np.float32)).astype(BF16)


def part_rows(box, rhs):
    start = 2 * box * rhs
    return slice(start, start + rhs), slice(start + rhs, start + 2 * rhs)


def encode_kernel(rhs, group, src_hbm, enc_hbm, out_ref, share_ref, src_ref, enc_ref, coded_ref, sem):
    copies = [
        pltpu.make_async_copy(src_hbm, src_ref, sem.at[0]),
        pltpu.make_async_copy(enc_hbm.at[0], enc_ref.at[0], sem.at[1]),
        pltpu.make_async_copy(enc_hbm.at[1], enc_ref.at[1], sem.at[2]),
    ]
    for copy in copies:
        copy.start()
    copies[0].wait()
    src = src_ref[...]
    part = src.shape[0] // lax.axis_size("dir")
    share_ref[...] = src_ref[pl.ds(pl.multiple_of(lax.axis_index("dir") * part, part), part), :]
    copies[1].wait()
    with_re = dot_nt(src, enc_ref[0])
    copies[2].wait()
    with_im = dot_nt(src, enc_ref[1])
    rows = src.shape[0] // rhs
    pieces = LANES // group
    for block in range(coded_ref.shape[0]):
        cols = slice(block * LANES, (block + 1) * LANES)
        for box in range(rows // 2):
            re, im = part_rows(box, rhs)
            coded_ref[block, re, :] = with_re[re, cols] - with_im[im, cols]
            coded_ref[block, im, :] = with_re[im, cols] + with_im[re, cols]
    for block in range(coded_ref.shape[0]):
        flat = coded_ref.at[block]
        for tile in range(rhs // pieces):
            parts = [flat[pl.ds(tile * pieces + n, rows, stride=rhs), :] for n in range(pieces)]
            for slot in range(pieces):
                lanes = slice(slot * group, (slot + 1) * group)
                out_ref[block * pieces + slot, :, tile * LANES : (tile + 1) * LANES] = jnp.concatenate(
                    [part[:, lanes] for part in parts], axis=1
                ).astype(BF16)


def table_kernel(
    grid_x, parts, share, list_ref, mask_ref, box_hbm, kern_hbm, cell_hbm, full_hbm,
    fwd_ref, inv_ref, spec_ref, order_ref, box_ref, kern_ref, cell_ref, full_ref, sem,
):
    copies = [
        pltpu.make_async_copy(box_hbm, box_ref, sem.at[0]),
        pltpu.make_async_copy(cell_hbm, cell_ref, sem.at[1]),
        pltpu.make_async_copy(kern_hbm, kern_ref, sem.at[2]),
        pltpu.make_async_copy(full_hbm, full_ref, sem.at[3]),
    ]
    for copy in copies:
        copy.start()
    list_slots(share, list_ref, mask_ref, order_ref)
    full_hi, full_lo = full_ref.at[0], full_ref.at[1]
    cell_hi, cell_lo = cell_ref.at[0], cell_ref.at[1]
    plane = full_hi.shape[0] // 2
    cells = GY * GZ
    count = box_ref.shape[1]
    boxes = count * parts
    copies[0].wait()
    copies[1].wait()
    same = lax.broadcasted_iota(jnp.int32, (boxes, count), 0) // parts == lax.broadcasted_iota(jnp.int32, (boxes, count), 1)
    cell_col = jnp.sum(jnp.where(same, box_ref[...], 0), axis=1, keepdims=True)
    spread = jnp.where(same, 1.0, 0.0).astype(BF16)
    cell_row = dot_nt(jnp.broadcast_to(box_ref[...], (8, count)).astype(BF16), spread)[:1].astype(jnp.int32)
    down = lax.broadcasted_iota(jnp.int32, (2 * cells, boxes), 0)
    part_row = lax.broadcasted_iota(jnp.int32, (2 * cells, boxes), 1) % 2
    across = lax.broadcasted_iota(jnp.int32, (boxes, 2 * cells), 1)
    part_col = lax.broadcasted_iota(jnp.int32, (boxes, 2 * cells), 0) % 2
    for x in range(grid_x):
        hit = (cell_row - x * cells + part_row * cells == down) & (cell_row // cells == x)
        place = jnp.where(hit, 1.0, 0.0).astype(BF16)
        fwd_ref[x, :, :boxes] = dot_nn(cell_hi[...], place).astype(BF16)
        fwd_ref[x, :, boxes:] = dot_nn(cell_lo[...], place).astype(BF16)
        hit = (cell_col - x * cells + part_col * cells == across) & (cell_col // cells == x)
        place = jnp.where(hit, 1.0 / plane, 0.0).astype(BF16)
        inv_ref[x, 0] = dot_nt(place, cell_hi[...]).astype(BF16)
        inv_ref[x, 1] = dot_nt(place, cell_lo[...]).astype(BF16)
    point = lax.broadcasted_iota(jnp.int32, (1, 2 * plane), 1) % plane
    off_y, off_z = point // (2 * GZ), point % (2 * GZ)
    close = ((off_y <= 1) | (off_y == 2 * GY - 1)) & ((off_z <= 1) | (off_z == 2 * GZ - 1))
    keep = jnp.where(close, 0.0, 1.0)
    copies[2].wait()
    copies[3].wait()
    repeat = LANES // kern_ref.shape[0]
    double_x = kern_ref.shape[2]
    for off in range(double_x):
        if off == grid_x:
            continue
        kept = jnp.concatenate([kern_ref[:, 0, off, :], kern_ref[:, 1, off, :]], axis=1)
        if off <= 1 or off == double_x - 1:
            kept = kept * keep
        high, low = split(kept)
        high = jnp.concatenate([high] * repeat, axis=0)
        low = jnp.concatenate([low] * repeat, axis=0)
        spec_ref[off] = dot_nt(full_hi[...], high) + dot_nt(full_hi[...], low) + dot_nt(full_lo[...], high)


def far_kernel(grid_x, coded_ref, fwd_ref, inv_ref, spec_ref, out_ref):
    owners, rows, width = coded_ref.shape
    plane = spec_ref.shape[1] // 2
    double_x = spec_ref.shape[0]
    step = min(2 * LANES, width)
    for start in range(0, width, step):
        cols = slice(start, start + step)
        coded = coded_ref[:, :, cols].reshape(owners * rows, step)
        coded = jnp.concatenate([coded, coded], axis=0)
        data = [dot_nn(fwd_ref[x], coded) for x in range(grid_x)]
        total = None
        for x in range(grid_x):
            tiles = []
            for tile in range(step // LANES):
                lanes = slice(tile * LANES, (tile + 1) * LANES)
                re = im = None
                for s in range(grid_x):
                    off = (x - s) % double_x
                    s_re, s_im = spec_ref[off, :plane], spec_ref[off, plane:]
                    d_re, d_im = data[s][:plane, lanes], data[s][plane:, lanes]
                    p_re = d_re * s_re - d_im * s_im
                    p_im = d_re * s_im + d_im * s_re
                    re = p_re if re is None else re + p_re
                    im = p_im if im is None else im + p_im
                tiles.append(jnp.concatenate([re, im], axis=0))
            high, low = split(jnp.concatenate(tiles, axis=1))
            term = dot_nn(inv_ref[x, 0], high) + dot_nn(inv_ref[x, 0], low) + dot_nn(inv_ref[x, 1], high)
            total = term if total is None else total + term
        out_ref[:, :, cols] = total.astype(BF16).reshape(owners, rows, step)


def list_slots(share, list_ref, mask_ref, order_ref):
    boxes, slots = list_ref.shape
    count = boxes * slots
    me, side = lax.axis_index("box"), lax.axis_index("dir")
    for box in range(boxes):

        def visit(slot, filled):
            valid = mask_ref[box, slot] != 0
            source = list_ref[box, slot]
            owner, place = lax.div(source, boxes), lax.rem(source, boxes)
            other = lax.div(place, share) != side
            rank = box * slots + jnp.where(other, filled[1] + count, filled[0])

            @pl.when(valid)
            def _():
                order_ref[rank] = (owner ^ me) * share + lax.rem(place, share)
                order_ref[2 * count + rank] = box * slots + slot

            return (
                filled[0] + (valid & ~other).astype(jnp.int32),
                filled[1] + (valid & other).astype(jnp.int32),
            )

        filled = lax.fori_loop(0, slots, visit, (jnp.int32(0), jnp.int32(0)))
        for half in range(2):
            order_ref[4 * count + half * boxes + box] = filled[half]

            @pl.loop(filled[half], slots)
            def _(rank):
                order_ref[half * count + box * slots + rank] = 0
                order_ref[(2 + half) * count + box * slots + rank] = count


def near_products(half, boxes, order_ref, src_ref, blk_ref, acc, arrived):
    count = blk_ref.shape[0] - 1
    slots = count // boxes

    def product(box, ranks):
        entries = [half * count + box * slots + rank for rank in ranks]
        places = [order_ref[2 * count + n] for n in entries]
        sources = [order_ref[n] for n in entries]
        vectors = jnp.concatenate([src_ref[lax.div(n, src_ref.shape[1]), lax.rem(n, src_ref.shape[1])] for n in sources], axis=1)
        return [
            dot_nt(vectors, jnp.concatenate([blk_ref[place, part] for place in places], axis=1)) for part in range(2)
        ]

    first = min(6, slots)
    for box in range(boxes):
        arrived(box)
        acc[box, 0], acc[box, 1] = product(box, range(first))
    for box in range(boxes):

        @pl.when(order_ref[4 * count + half * boxes + box] > first)
        def _():
            more = product(box, range(first, slots))
            acc[box, 0] += more[0]
            acc[box, 1] += more[1]


def near_mine_kernel(boxes, order_ref, src_ref, blocks_hbm, blk_ref, out_ref, acc, sem):
    count = blk_ref.shape[0] - 1
    slots = count // boxes

    def block_copy(half, box, rank):
        place = order_ref[(2 + half) * count + box * slots + rank]
        return pltpu.make_async_copy(
            blocks_hbm.at[box, place - box * slots], blk_ref.at[place], sem.at[half * boxes + box]
        )

    for half in range(2):
        for box in range(boxes):

            @pl.loop(0, order_ref[4 * count + half * boxes + box])
            def _(rank):
                block_copy(half, box, rank).start()

    blk_ref[count] = jnp.zeros(blk_ref.shape[1:], BF16)

    def arrived(half, box):
        @pl.loop(0, order_ref[4 * count + half * boxes + box])
        def _(rank):
            block_copy(half, box, rank).wait()

    near_products(0, boxes, order_ref, src_ref, blk_ref, acc, functools.partial(arrived, 0))
    for box in range(boxes):
        rows_re, rows_im, re, im = near_rows(box, acc.shape[2] // 2)
        out_ref[rows_re, :] = acc[box, 0, re, :] - acc[box, 1, im, :]
        out_ref[rows_im, :] = acc[box, 0, im, :] + acc[box, 1, re, :]
    for box in range(boxes):
        arrived(1, box)


def near_theirs_kernel(boxes, order_ref, src_ref, blk_ref, base_ref, out_ref, acc):
    near_products(1, boxes, order_ref, src_ref, blk_ref, acc, lambda box: None)
    for box in range(boxes):
        rows_re, rows_im, re, im = near_rows(box, acc.shape[2] // 2)
        out_ref[rows_re, :] = base_ref[rows_re, :] + (acc[box, 0, re, :] - acc[box, 1, im, :])
        out_ref[rows_im, :] = base_ref[rows_im, :] + (acc[box, 0, im, :] + acc[box, 1, re, :])


def near_rows(box, half):
    return (*part_rows(box, half), slice(0, half), slice(half, 2 * half))


def decode_kernel(rhs, group, far_ref, dec_ref, near_ref, own_ref, other_ref, wide, total):
    _, rows, width = far_ref.shape
    pieces = LANES // group
    for block in range(wide.shape[0]):
        flat = wide.at[block]
        for tile in range(width // LANES):
            cols = slice(tile * LANES, (tile + 1) * LANES)
            parts = [far_ref[block * pieces + slot, :, cols].astype(F32) for slot in range(pieces)]
            for n in range(pieces):
                lanes = slice(n * group, (n + 1) * group)
                flat[pl.ds(tile * pieces + n, rows, stride=rhs), :] = jnp.concatenate(
                    [part[:, lanes] for part in parts], axis=1
                )
    fields = jnp.concatenate([wide[block].astype(BF16) for block in range(wide.shape[0])], axis=1)
    with_re = dot_nn(fields, dec_ref[0])
    with_im = dot_nn(fields, dec_ref[1])
    for box in range(rows // 2):
        re, im = part_rows(box, rhs)
        total[re, :] = near_ref[re, :] + (with_re[re] - with_im[im])
        total[im, :] = near_ref[im, :] + (with_re[im] + with_im[re])
    half = total.shape[1] // 2
    first = lax.axis_index("dir") == 0
    left, right = total[:, :half], total[:, half:]
    own_ref[...] = jnp.where(first, left, right)
    other_ref[...] = jnp.where(first, right, left)


def join_kernel(*refs):
    for n, ref in enumerate(refs[:-1]):
        refs[-1][:, n] = ref[...]


def join(pieces):
    shape = pieces[0].shape
    joined = pl.pallas_call(
        join_kernel,
        out_shape=pltpu.VMEM((shape[0], len(pieces)) + shape[1:], pieces[0].dtype),
        in_specs=[vmem()] * len(pieces),
        out_specs=vmem(),
        compiler_params=budget(4),
        name="join",
    )(*pieces)
    return joined.reshape((-1,) + shape[1:])


def gather_shares(share):
    size = lax.axis_size("box")
    held = share[None]
    low = size
    while low > 1:
        fan = 4 if low % 4 == 0 else 2
        low //= fan
        moved = [held]
        for delta in range(1, fan):
            moved.append(lax.ppermute(held, "box", [(i, i ^ (delta * low)) for i in range(size)]))
        held = join(moved)
    return held


def budget(mebibytes):
    return pltpu.CompilerParams(vmem_limit_bytes=mebibytes << 20)


def stay(array):
    return pltpu.with_memory_space_constraint(array, pltpu.HBM)


def vmem():
    return pl.BlockSpec(memory_space=pltpu.VMEM)


def smem():
    return pl.BlockSpec(memory_space=pltpu.SMEM)


def hbm():
    return pl.BlockSpec(memory_space=pltpu.HBM)


def whole_product(sources, encode, kernel, decode, near_blocks, near_list, near_mask, box_cell):
    owners, sides = lax.axis_size("box"), lax.axis_size("dir")
    per_box, parts, rhs, unknowns = sources.shape
    group_dirs, _, double_x, plane = kernel.shape
    side_dirs = encode.shape[1]
    grid_x = double_x // 2
    rows = per_box * parts
    width = rhs * group_dirs
    boxes = box_cell.shape[0]

    share = per_box // sides
    coded, own_share = pl.pallas_call(
        functools.partial(encode_kernel, rhs, group_dirs),
        out_shape=(
            pltpu.VMEM((owners, rows, width), BF16),
            pltpu.VMEM((share * parts * rhs, unknowns), BF16),
        ),
        in_specs=[hbm(), hbm()],
        out_specs=(vmem(),) * 2,
        scratch_shapes=[
            pltpu.VMEM((rows * rhs, unknowns), BF16),
            pltpu.VMEM(encode.shape, BF16),
            pltpu.VMEM((side_dirs // LANES, rows * rhs, LANES), F32),
            pltpu.SemaphoreType.DMA((3,)),
        ],
        compiler_params=budget(8),
        name="encode",
    )(stay(sources.reshape(rows * rhs, unknowns)), stay(encode))
    arrived = lax.all_to_all(coded, "box", split_axis=0, concat_axis=0, tiled=True)
    mine = gather_shares(own_share.reshape(share, parts * rhs, unknowns))
    theirs = lax.ppermute(mine, "dir", [(i, 1 - i) for i in range(sides)])

    cell = np.arange(GY * GZ)
    cell_hi, cell_lo = plane_table(cell // GZ, cell % GZ)
    point = np.arange(plane)
    full_hi, full_lo = plane_table(point // (2 * GZ), point % (2 * GZ))
    constants = (np.stack([cell_hi, cell_lo]), np.stack([full_hi, full_lo]))
    count = per_box * near_list.shape[1]
    forward, inverse, spectrum, order = pl.pallas_call(
        functools.partial(table_kernel, grid_x, parts, share),
        out_shape=(
            pltpu.VMEM((grid_x, 2 * plane, 2 * parts * boxes), BF16),
            pltpu.VMEM((grid_x, 2, parts * boxes, 2 * plane), BF16),
            pltpu.VMEM((double_x, 2 * plane, LANES), F32),
            jax.ShapeDtypeStruct((4 * count + 2 * per_box,), jnp.int32),
        ),
        in_specs=[smem(), smem()] + [hbm()] * 4,
        out_specs=(vmem(), vmem(), vmem(), smem()),
        scratch_shapes=[
            pltpu.VMEM((1, boxes), jnp.int32),
            pltpu.VMEM(kernel.shape, F32),
            pltpu.VMEM(constants[0].shape, BF16),
            pltpu.VMEM(constants[1].shape, BF16),
            pltpu.SemaphoreType.DMA((4,)),
        ],
        compiler_params=budget(24),
        name="tables",
    )(stay(near_list), stay(near_mask), stay(box_cell[None, :]), stay(kernel), *[stay(jnp.asarray(table)) for table in constants])

    far = pl.pallas_call(
        functools.partial(far_kernel, grid_x),
        out_shape=pltpu.VMEM((owners, rows, width), BF16),
        in_specs=[vmem()] * 4,
        out_specs=vmem(),
        compiler_params=budget(8),
        name="far",
    )(arrived, forward, inverse, spectrum)
    returned = lax.all_to_all(far, "box", split_axis=0, concat_axis=0, tiled=True)


    near_acc = pltpu.VMEM((per_box, parts, parts * rhs, unknowns), F32)
    blocks, near_part = pl.pallas_call(
        functools.partial(near_mine_kernel, per_box),
        out_shape=(
            pltpu.VMEM((count + 1,) + near_blocks.shape[2:], BF16),
            pltpu.VMEM((rows * rhs, unknowns), F32),
        ),
        in_specs=[smem(), vmem(), hbm()],
        out_specs=(vmem(),) * 2,
        scratch_shapes=[near_acc, pltpu.SemaphoreType.DMA((2 * per_box,))],
        compiler_params=budget(4),
        name="near_mine",
    )(order, mine, stay(near_blocks))
    near_part = pl.pallas_call(
        functools.partial(near_theirs_kernel, per_box),
        out_shape=pltpu.VMEM((rows * rhs, unknowns), F32),
        in_specs=[smem(), vmem(), vmem(), vmem()],
        out_specs=vmem(),
        scratch_shapes=[near_acc],
        compiler_params=budget(4),
        name="near_theirs",
    )(order, theirs, blocks, near_part)

    half = unknowns // sides
    own, other = pl.pallas_call(
        functools.partial(decode_kernel, rhs, group_dirs),
        out_shape=(pltpu.VMEM((rows * rhs, half), F32),) * 2,
        in_specs=[vmem(), vmem(), vmem()],
        out_specs=(vmem(),) * 2,
        scratch_shapes=[
            pltpu.VMEM((side_dirs // LANES, rows * rhs, LANES), F32),
            pltpu.VMEM((rows * rhs, unknowns), F32),
        ],
        compiler_params=budget(8),
        name="decode",
    )(returned, decode, near_part)
    swapped = lax.ppermute(other, "dir", [(i, 1 - i) for i in range(sides)])
    return (own + swapped).reshape(per_box, parts, rhs, half)


def solution(mesh):
    in_specs = (
        P("box", None, None, None),
        P(None, "dir", None),
        P(("dir", "box"), None, None, None),
        P(None, "dir", None),
        P("box", "dir", None, None, None),
        P("box", "dir"),
        P("box", "dir"),
        P(),
    )
    out_specs = P("box", None, None, "dir")
    return jax.shard_map(whole_product, mesh=mesh, in_specs=in_specs, out_specs=out_specs, check_vma=False)
```

```python
import functools
import math

import jax
import jax.numpy as jnp
import numpy as np
from jax import lax
from jax.experimental import pallas as pl
from jax.experimental.pallas import tpu as pltpu
from jax.sharding import PartitionSpec as P


GY = 8
GZ = 4
LANES = 128

F32 = jnp.float32
BF16 = jnp.bfloat16


def dot_nt(left, right):
    return lax.dot_general(left, right, (((1,), (1,)), ((), ())), preferred_element_type=F32)


def dot_nn(left, right):
    return lax.dot_general(left, right, (((1,), (0,)), ((), ())), preferred_element_type=F32)


def split(value):
    high = value.astype(BF16)
    return high, (value - high.astype(F32)).astype(BF16)


def plane_table(points_y, points_z):
    freq = np.arange(4 * GY * GZ)
    turns = np.outer(freq // (2 * GZ), points_y) % (2 * GY) / (2 * GY)
    turns = turns + np.outer(freq % (2 * GZ), points_z) % (2 * GZ) / (2 * GZ)
    cosine, sine = np.cos(2.0 * math.pi * turns), np.sin(2.0 * math.pi * turns)
    table = np.block([[cosine, sine], [-sine, cosine]]).astype(np.float32)
    high = table.astype(BF16)
    return high, (table - high.astype(np.float32)).astype(BF16)


def part_rows(box, rhs):
    start = 2 * box * rhs
    return slice(start, start + rhs), slice(start + rhs, start + 2 * rhs)


def encode_kernel(rhs, group, src_hbm, enc_hbm, out_ref, whole_ref, share_ref, src_ref, enc_ref, coded_ref, sem):
    copies = [
        pltpu.make_async_copy(src_hbm, src_ref, sem.at[0]),
        pltpu.make_async_copy(enc_hbm.at[0], enc_ref.at[0], sem.at[1]),
        pltpu.make_async_copy(enc_hbm.at[1], enc_ref.at[1], sem.at[2]),
    ]
    for copy in copies:
        copy.start()
    copies[0].wait()
    src = src_ref[...]
    whole_ref[...] = src
    part = src.shape[0] // lax.axis_size("dir")
    share_ref[...] = src_ref[pl.ds(pl.multiple_of(lax.axis_index("dir") * part, part), part), :]
    copies[1].wait()
    with_re = dot_nt(src, enc_ref[0])
    copies[2].wait()
    with_im = dot_nt(src, enc_ref[1])
    rows = src.shape[0] // rhs
    pieces = LANES // group
    for block in range(coded_ref.shape[0]):
        cols = slice(block * LANES, (block + 1) * LANES)
        for box in range(rows // 2):
            re, im = part_rows(box, rhs)
            coded_ref[block, re, :] = with_re[re, cols] - with_im[im, cols]
            coded_ref[block, im, :] = with_re[im, cols] + with_im[re, cols]
    for block in range(coded_ref.shape[0]):
        flat = coded_ref.at[block]
        for tile in range(rhs // pieces):
            parts = [flat[pl.ds(tile * pieces + n, rows, stride=rhs), :] for n in range(pieces)]
            for slot in range(pieces):
                lanes = slice(slot * group, (slot + 1) * group)
                out_ref[block * pieces + slot, :, tile * LANES : (tile + 1) * LANES] = jnp.concatenate(
                    [part[:, lanes] for part in parts], axis=1
                ).astype(BF16)


def table_kernel(
    grid_x, parts, share, list_ref, mask_ref, box_hbm, kern_hbm, cell_hbm, full_hbm,
    fwd_ref, inv_ref, spec_ref, order_ref, box_ref, kern_ref, cell_ref, full_ref, sem,
):
    copies = [
        pltpu.make_async_copy(box_hbm, box_ref, sem.at[0]),
        pltpu.make_async_copy(cell_hbm, cell_ref, sem.at[1]),
        pltpu.make_async_copy(kern_hbm, kern_ref, sem.at[2]),
        pltpu.make_async_copy(full_hbm, full_ref, sem.at[3]),
    ]
    for copy in copies:
        copy.start()
    list_slots(share, list_ref, mask_ref, order_ref)
    full_hi, full_lo = full_ref.at[0], full_ref.at[1]
    cell_hi, cell_lo = cell_ref.at[0], cell_ref.at[1]
    plane = full_hi.shape[0] // 2
    cells = GY * GZ
    count = box_ref.shape[1]
    boxes = count * parts
    copies[0].wait()
    copies[1].wait()
    same = lax.broadcasted_iota(jnp.int32, (boxes, count), 0) // parts == lax.broadcasted_iota(jnp.int32, (boxes, count), 1)
    cell_col = jnp.sum(jnp.where(same, box_ref[...], 0), axis=1, keepdims=True)
    spread = jnp.where(same, 1.0, 0.0).astype(BF16)
    cell_row = dot_nt(jnp.broadcast_to(box_ref[...], (8, count)).astype(BF16), spread)[:1].astype(jnp.int32)
    down = lax.broadcasted_iota(jnp.int32, (2 * cells, boxes), 0)
    part_row = lax.broadcasted_iota(jnp.int32, (2 * cells, boxes), 1) % 2
    across = lax.broadcasted_iota(jnp.int32, (boxes, 2 * cells), 1)
    part_col = lax.broadcasted_iota(jnp.int32, (boxes, 2 * cells), 0) % 2
    for x in range(grid_x):
        hit = (cell_row - x * cells + part_row * cells == down) & (cell_row // cells == x)
        place = jnp.where(hit, 1.0, 0.0).astype(BF16)
        fwd_ref[x, :, :boxes] = dot_nn(cell_hi[...], place).astype(BF16)
        fwd_ref[x, :, boxes:] = dot_nn(cell_lo[...], place).astype(BF16)
        hit = (cell_col - x * cells + part_col * cells == across) & (cell_col // cells == x)
        place = jnp.where(hit, 1.0 / plane, 0.0).astype(BF16)
        inv_ref[x, 0] = dot_nt(place, cell_hi[...]).astype(BF16)
        inv_ref[x, 1] = dot_nt(place, cell_lo[...]).astype(BF16)
    point = lax.broadcasted_iota(jnp.int32, (1, 2 * plane), 1) % plane
    off_y, off_z = point // (2 * GZ), point % (2 * GZ)
    close = ((off_y <= 1) | (off_y == 2 * GY - 1)) & ((off_z <= 1) | (off_z == 2 * GZ - 1))
    keep = jnp.where(close, 0.0, 1.0)
    copies[2].wait()
    copies[3].wait()
    repeat = LANES // kern_ref.shape[0]
    double_x = kern_ref.shape[2]
    for off in range(double_x):
        if off == grid_x:
            continue
        kept = jnp.concatenate([kern_ref[:, 0, off, :], kern_ref[:, 1, off, :]], axis=1)
        if off <= 1 or off == double_x - 1:
            kept = kept * keep
        high, low = split(kept)
        high = jnp.concatenate([high] * repeat, axis=0)
        low = jnp.concatenate([low] * repeat, axis=0)
        spec_ref[off] = dot_nt(full_hi[...], high) + dot_nt(full_hi[...], low) + dot_nt(full_lo[...], high)


def far_kernel(grid_x, coded_ref, fwd_ref, inv_ref, spec_ref, out_ref):
    owners, rows, width = coded_ref.shape
    plane = spec_ref.shape[1] // 2
    double_x = spec_ref.shape[0]
    step = min(2 * LANES, width)
    for start in range(0, width, step):
        cols = slice(start, start + step)
        coded = coded_ref[:, :, cols].reshape(owners * rows, step)
        coded = jnp.concatenate([coded, coded], axis=0)
        data = [dot_nn(fwd_ref[x], coded) for x in range(grid_x)]
        total = None
        for x in range(grid_x):
            tiles = []
            for tile in range(step // LANES):
                lanes = slice(tile * LANES, (tile + 1) * LANES)
                re = im = None
                for s in range(grid_x):
                    off = (x - s) % double_x
                    s_re, s_im = spec_ref[off, :plane], spec_ref[off, plane:]
                    d_re, d_im = data[s][:plane, lanes], data[s][plane:, lanes]
                    p_re = d_re * s_re - d_im * s_im
                    p_im = d_re * s_im + d_im * s_re
                    re = p_re if re is None else re + p_re
                    im = p_im if im is None else im + p_im
                tiles.append(jnp.concatenate([re, im], axis=0))
            high, low = split(jnp.concatenate(tiles, axis=1))
            term = dot_nn(inv_ref[x, 0], high) + dot_nn(inv_ref[x, 0], low) + dot_nn(inv_ref[x, 1], high)
            total = term if total is None else total + term
        out_ref[:, :, cols] = total.astype(BF16).reshape(owners, rows, step)


def list_slots(share, list_ref, mask_ref, order_ref):
    boxes, slots = list_ref.shape
    count = boxes * slots
    me, side = lax.axis_index("box"), lax.axis_index("dir")
    rest = lax.axis_size("box") // 4
    for box in range(boxes):

        def visit(slot, filled):
            valid = mask_ref[box, slot] != 0
            source = list_ref[box, slot]
            owner, place = lax.div(source, boxes), lax.rem(source, boxes)
            apart = owner ^ me
            group, inner = lax.div(apart, rest), lax.rem(apart, rest)
            in_half, whole_share = lax.rem(place, share), (group == 1) | (group == 2)
            core = jnp.where(whole_share, group - 1, lax.div(place, share))
            entry = jnp.where(whole_share, share + place, in_half + jnp.where(group == 3, share + boxes, 0))
            other = core != side
            rank = box * slots + jnp.where(other, filled[1] + count, filled[0])

            @pl.when(valid)
            def _():
                order_ref[rank] = entry * rest + inner
                order_ref[2 * count + rank] = box * slots + slot

            return (
                filled[0] + (valid & ~other).astype(jnp.int32),
                filled[1] + (valid & other).astype(jnp.int32),
            )

        filled = lax.fori_loop(0, slots, visit, (jnp.int32(0), jnp.int32(0)))
        for half in range(2):
            order_ref[4 * count + half * boxes + box] = filled[half]

            @pl.loop(filled[half], slots)
            def _(rank):
                order_ref[half * count + box * slots + rank] = 0
                order_ref[(2 + half) * count + box * slots + rank] = count


def near_products(half, boxes, order_ref, src_ref, blk_ref, acc, arrived):
    count = blk_ref.shape[0] - 1
    slots = count // boxes

    def product(box, ranks):
        entries = [half * count + box * slots + rank for rank in ranks]
        places = [order_ref[2 * count + n] for n in entries]
        sources = [order_ref[n] for n in entries]
        vectors = jnp.concatenate([src_ref[n] for n in sources], axis=1)
        return [
            dot_nt(vectors, jnp.concatenate([blk_ref[place, part] for place in places], axis=1)) for part in range(2)
        ]

    first = min(6, slots)
    for box in range(boxes):
        arrived(box)
        acc[box, 0], acc[box, 1] = product(box, range(first))
    for box in range(boxes):

        @pl.when(order_ref[4 * count + half * boxes + box] > first)
        def _():
            more = product(box, range(first, slots))
            acc[box, 0] += more[0]
            acc[box, 1] += more[1]


def near_mine_kernel(boxes, order_ref, src_ref, blocks_hbm, blk_ref, out_ref, acc, sem):
    count = blk_ref.shape[0] - 1
    slots = count // boxes

    def block_copy(half, box, rank):
        place = order_ref[(2 + half) * count + box * slots + rank]
        return pltpu.make_async_copy(
            blocks_hbm.at[box, place - box * slots], blk_ref.at[place], sem.at[half * boxes + box]
        )

    for half in range(2):
        for box in range(boxes):

            @pl.loop(0, order_ref[4 * count + half * boxes + box])
            def _(rank):
                block_copy(half, box, rank).start()

    blk_ref[count] = jnp.zeros(blk_ref.shape[1:], BF16)

    def arrived(half, box):
        @pl.loop(0, order_ref[4 * count + half * boxes + box])
        def _(rank):
            block_copy(half, box, rank).wait()

    near_products(0, boxes, order_ref, src_ref, blk_ref, acc, functools.partial(arrived, 0))
    for box in range(boxes):
        rows_re, rows_im, re, im = near_rows(box, acc.shape[2] // 2)
        out_ref[rows_re, :] = acc[box, 0, re, :] - acc[box, 1, im, :]
        out_ref[rows_im, :] = acc[box, 0, im, :] + acc[box, 1, re, :]
    for box in range(boxes):
        arrived(1, box)


def near_theirs_kernel(boxes, order_ref, src_ref, blk_ref, base_ref, out_ref, acc):
    near_products(1, boxes, order_ref, src_ref, blk_ref, acc, lambda box: None)
    for box in range(boxes):
        rows_re, rows_im, re, im = near_rows(box, acc.shape[2] // 2)
        out_ref[rows_re, :] = base_ref[rows_re, :] + (acc[box, 0, re, :] - acc[box, 1, im, :])
        out_ref[rows_im, :] = base_ref[rows_im, :] + (acc[box, 0, im, :] + acc[box, 1, re, :])


def near_rows(box, half):
    return (*part_rows(box, half), slice(0, half), slice(half, 2 * half))


def decode_kernel(rhs, group, far_ref, dec_ref, near_ref, own_ref, other_ref, wide, total):
    _, rows, width = far_ref.shape
    pieces = LANES // group
    for block in range(wide.shape[0]):
        flat = wide.at[block]
        for tile in range(width // LANES):
            cols = slice(tile * LANES, (tile + 1) * LANES)
            parts = [far_ref[block * pieces + slot, :, cols].astype(F32) for slot in range(pieces)]
            for n in range(pieces):
                lanes = slice(n * group, (n + 1) * group)
                flat[pl.ds(tile * pieces + n, rows, stride=rhs), :] = jnp.concatenate(
                    [part[:, lanes] for part in parts], axis=1
                )
    fields = jnp.concatenate([wide[block].astype(BF16) for block in range(wide.shape[0])], axis=1)
    with_re = dot_nn(fields, dec_ref[0])
    with_im = dot_nn(fields, dec_ref[1])
    for box in range(rows // 2):
        re, im = part_rows(box, rhs)
        total[re, :] = near_ref[re, :] + (with_re[re] - with_im[im])
        total[im, :] = near_ref[im, :] + (with_re[im] + with_im[re])
    half = total.shape[1] // 2
    first = lax.axis_index("dir") == 0
    left, right = total[:, :half], total[:, half:]
    own_ref[...] = jnp.where(first, left, right)
    other_ref[...] = jnp.where(first, right, left)


def stack_kernel(*refs):
    for n, ref in enumerate(refs[:-1]):
        refs[-1][:, n] = ref[...]


def lay_kernel(*refs):
    start = 0
    for ref in refs[:-1]:
        refs[-1][start : start + ref.shape[0]] = ref[...]
        start += ref.shape[0]


def join(kernel, pieces, shape):
    return pl.pallas_call(
        kernel,
        out_shape=pltpu.VMEM(shape, pieces[0].dtype),
        in_specs=[vmem()] * len(pieces),
        out_specs=vmem(),
        compiler_params=budget(4),
        name="join",
    )(*pieces)


def gather_shares(boxes, share):
    size = lax.axis_size("box")
    rest = size // 4
    pairs = [(2 * i + core, 2 * (i ^ ((core + 1) * rest)) + core) for i in range(size) for core in range(2)]
    whole = lax.ppermute(boxes, ("box", "dir"), pairs)
    third = lax.ppermute(share, "box", [(i, i ^ (3 * rest)) for i in range(size)])
    count = 2 * share.shape[0] + boxes.shape[0]
    held = join(lay_kernel, [share, whole, third], (count,) + share.shape[1:])
    while rest > 1:
        fan = 4 if rest % 4 == 0 else 2
        rest //= fan
        moved = [held]
        for delta in range(1, fan):
            moved.append(lax.ppermute(held, "box", [(i, i ^ (delta * rest)) for i in range(size)]))
        count *= fan
        held = join(stack_kernel, moved, (held.shape[0], fan) + share.shape[1:]).reshape((count,) + share.shape[1:])
    return held


def budget(mebibytes):
    return pltpu.CompilerParams(vmem_limit_bytes=mebibytes << 20)


def stay(array):
    return pltpu.with_memory_space_constraint(array, pltpu.HBM)


def vmem():
    return pl.BlockSpec(memory_space=pltpu.VMEM)


def smem():
    return pl.BlockSpec(memory_space=pltpu.SMEM)


def hbm():
    return pl.BlockSpec(memory_space=pltpu.HBM)


def whole_product(sources, encode, kernel, decode, near_blocks, near_list, near_mask, box_cell):
    owners, sides = lax.axis_size("box"), lax.axis_size("dir")
    per_box, parts, rhs, unknowns = sources.shape
    group_dirs, _, double_x, plane = kernel.shape
    side_dirs = encode.shape[1]
    grid_x = double_x // 2
    rows = per_box * parts
    width = rhs * group_dirs
    boxes = box_cell.shape[0]

    share = per_box // sides
    coded, own_boxes, own_share = pl.pallas_call(
        functools.partial(encode_kernel, rhs, group_dirs),
        out_shape=(
            pltpu.VMEM((owners, rows, width), BF16),
            pltpu.VMEM((per_box * parts * rhs, unknowns), BF16),
            pltpu.VMEM((share * parts * rhs, unknowns), BF16),
        ),
        in_specs=[hbm(), hbm()],
        out_specs=(vmem(),) * 3,
        scratch_shapes=[
            pltpu.VMEM((rows * rhs, unknowns), BF16),
            pltpu.VMEM(encode.shape, BF16),
            pltpu.VMEM((side_dirs // LANES, rows * rhs, LANES), F32),
            pltpu.SemaphoreType.DMA((3,)),
        ],
        compiler_params=budget(8),
        name="encode",
    )(stay(sources.reshape(rows * rhs, unknowns)), stay(encode))
    arrived = lax.all_to_all(coded, "box", split_axis=0, concat_axis=0, tiled=True)
    mine = gather_shares(own_boxes.reshape(per_box, parts * rhs, unknowns), own_share.reshape(share, parts * rhs, unknowns))
    theirs = lax.ppermute(mine, "dir", [(i, 1 - i) for i in range(sides)])

    cell = np.arange(GY * GZ)
    cell_hi, cell_lo = plane_table(cell // GZ, cell % GZ)
    point = np.arange(plane)
    full_hi, full_lo = plane_table(point // (2 * GZ), point % (2 * GZ))
    constants = (np.stack([cell_hi, cell_lo]), np.stack([full_hi, full_lo]))
    count = per_box * near_list.shape[1]
    forward, inverse, spectrum, order = pl.pallas_call(
        functools.partial(table_kernel, grid_x, parts, share),
        out_shape=(
            pltpu.VMEM((grid_x, 2 * plane, 2 * parts * boxes), BF16),
            pltpu.VMEM((grid_x, 2, parts * boxes, 2 * plane), BF16),
            pltpu.VMEM((double_x, 2 * plane, LANES), F32),
            jax.ShapeDtypeStruct((4 * count + 2 * per_box,), jnp.int32),
        ),
        in_specs=[smem(), smem()] + [hbm()] * 4,
        out_specs=(vmem(), vmem(), vmem(), smem()),
        scratch_shapes=[
            pltpu.VMEM((1, boxes), jnp.int32),
            pltpu.VMEM(kernel.shape, F32),
            pltpu.VMEM(constants[0].shape, BF16),
            pltpu.VMEM(constants[1].shape, BF16),
            pltpu.SemaphoreType.DMA((4,)),
        ],
        compiler_params=budget(24),
        name="tables",
    )(stay(near_list), stay(near_mask), stay(box_cell[None, :]), stay(kernel), *[stay(jnp.asarray(table)) for table in constants])

    far = pl.pallas_call(
        functools.partial(far_kernel, grid_x),
        out_shape=pltpu.VMEM((owners, rows, width), BF16),
        in_specs=[vmem()] * 4,
        out_specs=vmem(),
        compiler_params=budget(8),
        name="far",
    )(arrived, forward, inverse, spectrum)
    returned = lax.all_to_all(far, "box", split_axis=0, concat_axis=0, tiled=True)


    near_acc = pltpu.VMEM((per_box, parts, parts * rhs, unknowns), F32)
    blocks, near_part = pl.pallas_call(
        functools.partial(near_mine_kernel, per_box),
        out_shape=(
            pltpu.VMEM((count + 1,) + near_blocks.shape[2:], BF16),
            pltpu.VMEM((rows * rhs, unknowns), F32),
        ),
        in_specs=[smem(), vmem(), hbm()],
        out_specs=(vmem(),) * 2,
        scratch_shapes=[near_acc, pltpu.SemaphoreType.DMA((2 * per_box,))],
        compiler_params=budget(4),
        name="near_mine",
    )(order, mine, stay(near_blocks))
    near_part = pl.pallas_call(
        functools.partial(near_theirs_kernel, per_box),
        out_shape=pltpu.VMEM((rows * rhs, unknowns), F32),
        in_specs=[smem(), vmem(), vmem(), vmem()],
        out_specs=vmem(),
        scratch_shapes=[near_acc],
        compiler_params=budget(4),
        name="near_theirs",
    )(order, theirs, blocks, near_part)

    half = unknowns // sides
    own, other = pl.pallas_call(
        functools.partial(decode_kernel, rhs, group_dirs),
        out_shape=(pltpu.VMEM((rows * rhs, half), F32),) * 2,
        in_specs=[vmem(), vmem(), vmem()],
        out_specs=(vmem(),) * 2,
        scratch_shapes=[
            pltpu.VMEM((side_dirs // LANES, rows * rhs, LANES), F32),
            pltpu.VMEM((rows * rhs, unknowns), F32),
        ],
        compiler_params=budget(8),
        name="decode",
    )(returned, decode, near_part)
    swapped = lax.ppermute(other, "dir", [(i, 1 - i) for i in range(sides)])
    return (own + swapped).reshape(per_box, parts, rhs, half)


def solution(mesh):
    in_specs = (
        P("box", None, None, None),
        P(None, "dir", None),
        P(("dir", "box"), None, None, None),
        P(None, "dir", None),
        P("box", "dir", None, None, None),
        P("box", "dir"),
        P("box", "dir"),
        P(),
    )
    out_specs = P("box", None, None, "dir")
    return jax.shard_map(whole_product, mesh=mesh, in_specs=in_specs, out_specs=out_specs, check_vma=False)
```

```python
import functools
import math

import jax
import jax.numpy as jnp
import numpy as np
from jax import lax
from jax.experimental import pallas as pl
from jax.experimental.pallas import tpu as pltpu
from jax.sharding import PartitionSpec as P


GY = 8
GZ = 4
LANES = 128
PACK = 1 << 16

F32 = jnp.float32
BF16 = jnp.bfloat16


def dot_nt(left, right):
    return lax.dot_general(left, right, (((1,), (1,)), ((), ())), preferred_element_type=F32)


def dot_nn(left, right):
    return lax.dot_general(left, right, (((1,), (0,)), ((), ())), preferred_element_type=F32)


def split(value):
    high = value.astype(BF16)
    return high, (value - high.astype(F32)).astype(BF16)


def plane_table(points_y, points_z):
    freq = np.arange(4 * GY * GZ)
    turns = np.outer(freq // (2 * GZ), points_y) % (2 * GY) / (2 * GY)
    turns = turns + np.outer(freq % (2 * GZ), points_z) % (2 * GZ) / (2 * GZ)
    cosine, sine = np.cos(2.0 * math.pi * turns), np.sin(2.0 * math.pi * turns)
    table = np.block([[cosine, sine], [-sine, cosine]]).astype(np.float32)
    high = table.astype(BF16)
    return high, (table - high.astype(np.float32)).astype(BF16)


def part_rows(box, rhs):
    start = 2 * box * rhs
    return slice(start, start + rhs), slice(start + rhs, start + 2 * rhs)


def encode_kernel(rhs, group, src_hbm, enc_hbm, out_ref, whole_ref, share_ref, src_ref, enc_ref, coded_ref, sem):
    copies = [
        pltpu.make_async_copy(src_hbm, src_ref, sem.at[0]),
        pltpu.make_async_copy(enc_hbm.at[0], enc_ref.at[0], sem.at[1]),
        pltpu.make_async_copy(enc_hbm.at[1], enc_ref.at[1], sem.at[2]),
    ]
    for copy in copies:
        copy.start()
    copies[0].wait()
    src = src_ref[...]
    whole_ref[...] = src
    part = src.shape[0] // lax.axis_size("dir")
    share_ref[...] = src_ref[pl.ds(pl.multiple_of(lax.axis_index("dir") * part, part), part), :]
    copies[1].wait()
    with_re = dot_nt(src, enc_ref[0])
    copies[2].wait()
    with_im = dot_nt(src, enc_ref[1])
    rows = src.shape[0] // rhs
    pieces = LANES // group
    for block in range(coded_ref.shape[0]):
        cols = slice(block * LANES, (block + 1) * LANES)
        for box in range(rows // 2):
            re, im = part_rows(box, rhs)
            coded_ref[block, re, :] = with_re[re, cols] - with_im[im, cols]
            coded_ref[block, im, :] = with_re[im, cols] + with_im[re, cols]
    for block in range(coded_ref.shape[0]):
        flat = coded_ref.at[block]
        for tile in range(rhs // pieces):
            parts = [flat[pl.ds(tile * pieces + n, rows, stride=rhs), :] for n in range(pieces)]
            for slot in range(pieces):
                lanes = slice(slot * group, (slot + 1) * group)
                out_ref[block * pieces + slot, :, tile * LANES : (tile + 1) * LANES] = jnp.concatenate(
                    [part[:, lanes] for part in parts], axis=1
                ).astype(BF16)


def table_kernel(
    grid_x, parts, share, list_hbm, mask_hbm, box_hbm, kern_hbm, cell_hbm, full_hbm,
    fwd_ref, inv_ref, spec_ref, order_ref, list_ref, mask_ref, box_ref, kern_ref, cell_ref, full_ref, sem,
):
    copies = [
        pltpu.make_async_copy(box_hbm, box_ref, sem.at[0]),
        pltpu.make_async_copy(cell_hbm, cell_ref, sem.at[1]),
        pltpu.make_async_copy(kern_hbm, kern_ref, sem.at[2]),
        pltpu.make_async_copy(full_hbm, full_ref, sem.at[3]),
        pltpu.make_async_copy(list_hbm, list_ref, sem.at[4]),
        pltpu.make_async_copy(mask_hbm, mask_ref, sem.at[5]),
    ]
    for copy in copies:
        copy.start()
    copies[4].wait()
    copies[5].wait()
    list_slots(share, list_ref[...], mask_ref[...], order_ref)
    full_hi, full_lo = full_ref.at[0], full_ref.at[1]
    cell_hi, cell_lo = cell_ref.at[0], cell_ref.at[1]
    plane = full_hi.shape[0] // 2
    cells = GY * GZ
    count = box_ref.shape[1]
    boxes = count * parts
    copies[0].wait()
    copies[1].wait()
    same = lax.broadcasted_iota(jnp.int32, (boxes, count), 0) // parts == lax.broadcasted_iota(jnp.int32, (boxes, count), 1)
    cell_col = jnp.sum(jnp.where(same, box_ref[...], 0), axis=1, keepdims=True)
    spread = jnp.where(same, 1.0, 0.0).astype(BF16)
    cell_row = dot_nt(jnp.broadcast_to(box_ref[...], (8, count)).astype(BF16), spread)[:1].astype(jnp.int32)
    down = lax.broadcasted_iota(jnp.int32, (2 * cells, boxes), 0)
    part_row = lax.broadcasted_iota(jnp.int32, (2 * cells, boxes), 1) % 2
    across = lax.broadcasted_iota(jnp.int32, (boxes, 2 * cells), 1)
    part_col = lax.broadcasted_iota(jnp.int32, (boxes, 2 * cells), 0) % 2
    for x in range(grid_x):
        hit = (cell_row - x * cells + part_row * cells == down) & (cell_row // cells == x)
        place = jnp.where(hit, 1.0, 0.0).astype(BF16)
        fwd_ref[x, :, :boxes] = dot_nn(cell_hi[...], place).astype(BF16)
        fwd_ref[x, :, boxes:] = dot_nn(cell_lo[...], place).astype(BF16)
        hit = (cell_col - x * cells + part_col * cells == across) & (cell_col // cells == x)
        place = jnp.where(hit, 1.0 / plane, 0.0).astype(BF16)
        inv_ref[x, 0] = dot_nt(place, cell_hi[...]).astype(BF16)
        inv_ref[x, 1] = dot_nt(place, cell_lo[...]).astype(BF16)
    point = lax.broadcasted_iota(jnp.int32, (1, 2 * plane), 1) % plane
    off_y, off_z = point // (2 * GZ), point % (2 * GZ)
    close = ((off_y <= 1) | (off_y == 2 * GY - 1)) & ((off_z <= 1) | (off_z == 2 * GZ - 1))
    keep = jnp.where(close, 0.0, 1.0)
    copies[2].wait()
    copies[3].wait()
    repeat = LANES // kern_ref.shape[0]
    double_x = kern_ref.shape[2]
    for off in range(double_x):
        if off == grid_x:
            continue
        kept = jnp.concatenate([kern_ref[:, 0, off, :], kern_ref[:, 1, off, :]], axis=1)
        if off <= 1 or off == double_x - 1:
            kept = kept * keep
        high, low = split(kept)
        high = jnp.concatenate([high] * repeat, axis=0)
        low = jnp.concatenate([low] * repeat, axis=0)
        spec_ref[off] = dot_nt(full_hi[...], high) + dot_nt(full_hi[...], low) + dot_nt(full_lo[...], high)


def far_kernel(grid_x, coded_ref, fwd_ref, inv_ref, spec_ref, out_ref):
    owners, rows, width = coded_ref.shape
    plane = spec_ref.shape[1] // 2
    double_x = spec_ref.shape[0]
    step = min(2 * LANES, width)
    for start in range(0, width, step):
        cols = slice(start, start + step)
        coded = coded_ref[:, :, cols].reshape(owners * rows, step)
        coded = jnp.concatenate([coded, coded], axis=0)
        data = [dot_nn(fwd_ref[x], coded) for x in range(grid_x)]
        total = None
        for x in range(grid_x):
            tiles = []
            for tile in range(step // LANES):
                lanes = slice(tile * LANES, (tile + 1) * LANES)
                re = im = None
                for s in range(grid_x):
                    off = (x - s) % double_x
                    s_re, s_im = spec_ref[off, :plane], spec_ref[off, plane:]
                    d_re, d_im = data[s][:plane, lanes], data[s][plane:, lanes]
                    p_re = d_re * s_re - d_im * s_im
                    p_im = d_re * s_im + d_im * s_re
                    re = p_re if re is None else re + p_re
                    im = p_im if im is None else im + p_im
                tiles.append(jnp.concatenate([re, im], axis=0))
            high, low = split(jnp.concatenate(tiles, axis=1))
            term = dot_nn(inv_ref[x, 0], high) + dot_nn(inv_ref[x, 0], low) + dot_nn(inv_ref[x, 1], high)
            total = term if total is None else total + term
        out_ref[:, :, cols] = total.astype(BF16).reshape(owners, rows, step)


def list_slots(share, near_list, near_mask, order_ref):
    boxes, slots = near_list.shape
    me, side = lax.axis_index("box"), lax.axis_index("dir")
    rest = lax.axis_size("box") // 4
    source = jnp.concatenate([near_list, near_list], axis=0)
    valid = jnp.concatenate([near_mask, near_mask], axis=0) != 0
    apart, place = (source // boxes) ^ me, source % boxes
    group, inner = apart // rest, apart % rest
    in_half, whole_share = place % share, group >= 2
    core = jnp.where(whole_share, 3 - group, place // share)
    entry = jnp.where(whole_share, share + place, in_half + jnp.where(group == 1, share + boxes, 0)) * rest + inner
    row = lax.broadcasted_iota(jnp.int32, source.shape, 0)
    used = jnp.where(valid & ((core == side) == (row < boxes)), 1, 0)
    rank = lax.broadcasted_iota(jnp.int32, order_ref.shape, 1)
    entry = entry + (row % boxes) * (slots * PACK)
    order = jnp.full_like(rank, boxes * slots * PACK)
    filled = jnp.zeros((2 * boxes, 1), jnp.int32)
    for slot in range(slots):
        here = used[:, slot : slot + 1]
        hit = (rank == filled) & (here != 0)
        order = jnp.where(hit, entry[:, slot : slot + 1] + slot * PACK, order)
        filled = filled + here
    order_ref[...] = jnp.where(rank == slots, filled, order)


def near_products(half, boxes, order_ref, src_ref, blk_ref, acc, arrived):
    count = blk_ref.shape[0] - 1
    slots = count // boxes

    def product(box, ranks):
        row = half * boxes + box
        packed = [order_ref[row, rank] for rank in ranks]
        places = [lax.div(entry, PACK) for entry in packed]
        sources = [lax.rem(entry, PACK) for entry in packed]
        vectors = jnp.concatenate([src_ref[n] for n in sources], axis=1)
        return [
            dot_nt(vectors, jnp.concatenate([blk_ref[place, part] for place in places], axis=1)) for part in range(2)
        ]

    first = min(5, slots)
    for box in range(boxes):
        arrived(box)
        acc[box, 0], acc[box, 1] = product(box, range(first))
    for start in range(first, slots, 3):
        for box in range(boxes):

            @pl.when(order_ref[half * boxes + box, slots] > start)
            def _():
                more = product(box, range(start, min(start + 3, slots)))
                acc[box, 0] += more[0]
                acc[box, 1] += more[1]


def near_mine_kernel(boxes, order_ref, src_ref, blocks_hbm, blk_ref, out_ref, acc, sem):
    count = blk_ref.shape[0] - 1
    slots = count // boxes

    def block_copy(half, box, rank):
        place = lax.div(order_ref[half * boxes + box, rank], PACK)
        return pltpu.make_async_copy(
            blocks_hbm.at[box, place - box * slots], blk_ref.at[place], sem.at[half * boxes + box]
        )

    for half in range(2):
        for box in range(boxes):

            @pl.loop(0, order_ref[half * boxes + box, slots])
            def _(rank):
                block_copy(half, box, rank).start()

    blk_ref[count] = jnp.zeros(blk_ref.shape[1:], BF16)

    def arrived(half, box):
        @pl.loop(0, order_ref[half * boxes + box, slots])
        def _(rank):
            block_copy(half, box, rank).wait()

    near_products(0, boxes, order_ref, src_ref, blk_ref, acc, functools.partial(arrived, 0))
    for box in range(boxes):
        rows_re, rows_im, re, im = near_rows(box, acc.shape[2] // 2)
        out_ref[rows_re, :] = acc[box, 0, re, :] - acc[box, 1, im, :]
        out_ref[rows_im, :] = acc[box, 0, im, :] + acc[box, 1, re, :]
    for box in range(boxes):
        arrived(1, box)


def near_theirs_kernel(boxes, order_ref, src_ref, blk_ref, base_ref, out_ref, acc):
    near_products(1, boxes, order_ref, src_ref, blk_ref, acc, lambda box: None)
    for box in range(boxes):
        rows_re, rows_im, re, im = near_rows(box, acc.shape[2] // 2)
        out_ref[rows_re, :] = base_ref[rows_re, :] + (acc[box, 0, re, :] - acc[box, 1, im, :])
        out_ref[rows_im, :] = base_ref[rows_im, :] + (acc[box, 0, im, :] + acc[box, 1, re, :])


def near_rows(box, half):
    return (*part_rows(box, half), slice(0, half), slice(half, 2 * half))


def decode_kernel(rhs, group, far_ref, dec_ref, near_ref, own_ref, other_ref, wide, total):
    _, rows, width = far_ref.shape
    pieces = LANES // group
    for block in range(wide.shape[0]):
        flat = wide.at[block]
        for tile in range(width // LANES):
            cols = slice(tile * LANES, (tile + 1) * LANES)
            parts = [far_ref[block * pieces + slot, :, cols].astype(F32) for slot in range(pieces)]
            for n in range(pieces):
                lanes = slice(n * group, (n + 1) * group)
                flat[pl.ds(tile * pieces + n, rows, stride=rhs), :] = jnp.concatenate(
                    [part[:, lanes] for part in parts], axis=1
                )
    fields = jnp.concatenate([wide[block].astype(BF16) for block in range(wide.shape[0])], axis=1)
    with_re = dot_nn(fields, dec_ref[0])
    with_im = dot_nn(fields, dec_ref[1])
    for box in range(rows // 2):
        re, im = part_rows(box, rhs)
        total[re, :] = near_ref[re, :] + (with_re[re] - with_im[im])
        total[im, :] = near_ref[im, :] + (with_re[im] + with_im[re])
    half = total.shape[1] // 2
    first = lax.axis_index("dir") == 0
    left, right = total[:, :half], total[:, half:]
    own_ref[...] = jnp.where(first, left, right)
    other_ref[...] = jnp.where(first, right, left)


def stack_kernel(*refs):
    for n, ref in enumerate(refs[:-1]):
        refs[-1][:, n] = ref[...]


def lay_kernel(*refs):
    start = 0
    for ref in refs[:-1]:
        refs[-1][start : start + ref.shape[0]] = ref[...]
        start += ref.shape[0]


def join(kernel, pieces, shape):
    return pl.pallas_call(
        kernel,
        out_shape=pltpu.VMEM(shape, pieces[0].dtype),
        in_specs=[vmem()] * len(pieces),
        out_specs=vmem(),
        compiler_params=budget(4),
        name="join",
    )(*pieces)


def gather_shares(boxes, share):
    size = lax.axis_size("box")
    rest = size // 4
    pairs = [(2 * i + core, 2 * (i ^ ((3 - core) * rest)) + core) for i in range(size) for core in range(2)]
    whole = lax.ppermute(boxes, ("box", "dir"), pairs)
    third = lax.ppermute(share, "box", [(i, i ^ rest) for i in range(size)])
    count = 2 * share.shape[0] + boxes.shape[0]
    held = join(lay_kernel, [share, whole, third], (count,) + share.shape[1:])
    while rest > 1:
        fan = 4 if rest % 4 == 0 else 2
        rest //= fan
        moved = [held]
        for delta in range(1, fan):
            moved.append(lax.ppermute(held, "box", [(i, i ^ (delta * rest)) for i in range(size)]))
        count *= fan
        held = join(stack_kernel, moved, (held.shape[0], fan) + share.shape[1:]).reshape((count,) + share.shape[1:])
    return held


def budget(mebibytes):
    return pltpu.CompilerParams(vmem_limit_bytes=mebibytes << 20)


def stay(array):
    return pltpu.with_memory_space_constraint(array, pltpu.HBM)


def vmem():
    return pl.BlockSpec(memory_space=pltpu.VMEM)


def smem():
    return pl.BlockSpec(memory_space=pltpu.SMEM)


def hbm():
    return pl.BlockSpec(memory_space=pltpu.HBM)


def whole_product(sources, encode, kernel, decode, near_blocks, near_list, near_mask, box_cell):
    owners, sides = lax.axis_size("box"), lax.axis_size("dir")
    per_box, parts, rhs, unknowns = sources.shape
    group_dirs, _, double_x, plane = kernel.shape
    side_dirs = encode.shape[1]
    grid_x = double_x // 2
    rows = per_box * parts
    width = rhs * group_dirs
    boxes = box_cell.shape[0]

    share = per_box // sides
    coded, own_boxes, own_share = pl.pallas_call(
        functools.partial(encode_kernel, rhs, group_dirs),
        out_shape=(
            pltpu.VMEM((owners, rows, width), BF16),
            pltpu.VMEM((per_box * parts * rhs, unknowns), BF16),
            pltpu.VMEM((share * parts * rhs, unknowns), BF16),
        ),
        in_specs=[hbm(), hbm()],
        out_specs=(vmem(),) * 3,
        scratch_shapes=[
            pltpu.VMEM((rows * rhs, unknowns), BF16),
            pltpu.VMEM(encode.shape, BF16),
            pltpu.VMEM((side_dirs // LANES, rows * rhs, LANES), F32),
            pltpu.SemaphoreType.DMA((3,)),
        ],
        compiler_params=budget(8),
        name="encode",
    )(stay(sources.reshape(rows * rhs, unknowns)), stay(encode))
    arrived = lax.all_to_all(coded, "box", split_axis=0, concat_axis=0, tiled=True)
    mine = gather_shares(own_boxes.reshape(per_box, parts * rhs, unknowns), own_share.reshape(share, parts * rhs, unknowns))
    theirs = lax.ppermute(mine, "dir", [(i, 1 - i) for i in range(sides)])

    cell = np.arange(GY * GZ)
    cell_hi, cell_lo = plane_table(cell // GZ, cell % GZ)
    point = np.arange(plane)
    full_hi, full_lo = plane_table(point // (2 * GZ), point % (2 * GZ))
    constants = (np.stack([cell_hi, cell_lo]), np.stack([full_hi, full_lo]))
    count = per_box * near_list.shape[1]
    forward, inverse, spectrum, order = pl.pallas_call(
        functools.partial(table_kernel, grid_x, parts, share),
        out_shape=(
            pltpu.VMEM((grid_x, 2 * plane, 2 * parts * boxes), BF16),
            pltpu.VMEM((grid_x, 2, parts * boxes, 2 * plane), BF16),
            pltpu.VMEM((double_x, 2 * plane, LANES), F32),
            jax.ShapeDtypeStruct((2 * per_box, LANES), jnp.int32),
        ),
        in_specs=[hbm()] * 6,
        out_specs=(vmem(),) * 4,
        scratch_shapes=[
            pltpu.VMEM(near_list.shape, jnp.int32),
            pltpu.VMEM(near_mask.shape, jnp.int32),
            pltpu.VMEM((1, boxes), jnp.int32),
            pltpu.VMEM(kernel.shape, F32),
            pltpu.VMEM(constants[0].shape, BF16),
            pltpu.VMEM(constants[1].shape, BF16),
            pltpu.SemaphoreType.DMA((6,)),
        ],
        compiler_params=budget(24),
        name="tables",
    )(stay(near_list), stay(near_mask), stay(box_cell[None, :]), stay(kernel), *[stay(jnp.asarray(table)) for table in constants])

    far = pl.pallas_call(
        functools.partial(far_kernel, grid_x),
        out_shape=pltpu.VMEM((owners, rows, width), BF16),
        in_specs=[vmem()] * 4,
        out_specs=vmem(),
        compiler_params=budget(8),
        name="far",
    )(arrived, forward, inverse, spectrum)
    returned = lax.all_to_all(far, "box", split_axis=0, concat_axis=0, tiled=True)


    near_acc = pltpu.VMEM((per_box, parts, parts * rhs, unknowns), F32)
    blocks, near_part = pl.pallas_call(
        functools.partial(near_mine_kernel, per_box),
        out_shape=(
            pltpu.VMEM((count + 1,) + near_blocks.shape[2:], BF16),
            pltpu.VMEM((rows * rhs, unknowns), F32),
        ),
        in_specs=[smem(), vmem(), hbm()],
        out_specs=(vmem(),) * 2,
        scratch_shapes=[near_acc, pltpu.SemaphoreType.DMA((2 * per_box,))],
        compiler_params=budget(4),
        name="near_mine",
    )(order, mine, stay(near_blocks))
    near_part = pl.pallas_call(
        functools.partial(near_theirs_kernel, per_box),
        out_shape=pltpu.VMEM((rows * rhs, unknowns), F32),
        in_specs=[smem(), vmem(), vmem(), vmem()],
        out_specs=vmem(),
        scratch_shapes=[near_acc],
        compiler_params=budget(4),
        name="near_theirs",
    )(order, theirs, blocks, near_part)

    half = unknowns // sides
    own, other = pl.pallas_call(
        functools.partial(decode_kernel, rhs, group_dirs),
        out_shape=(pltpu.VMEM((rows * rhs, half), F32),) * 2,
        in_specs=[vmem(), vmem(), vmem()],
        out_specs=(vmem(),) * 2,
        scratch_shapes=[
            pltpu.VMEM((side_dirs // LANES, rows * rhs, LANES), F32),
            pltpu.VMEM((rows * rhs, unknowns), F32),
        ],
        compiler_params=budget(8),
        name="decode",
    )(returned, decode, near_part)
    swapped = lax.ppermute(other, "dir", [(i, 1 - i) for i in range(sides)])
    return (own + swapped).reshape(per_box, parts, rhs, half)


def solution(mesh):
    in_specs = (
        P("box", None, None, None),
        P(None, "dir", None),
        P(("dir", "box"), None, None, None),
        P(None, "dir", None),
        P("box", "dir", None, None, None),
        P("box", "dir"),
        P("box", "dir"),
        P(),
    )
    out_specs = P("box", None, None, "dir")
    return jax.shard_map(whole_product, mesh=mesh, in_specs=in_specs, out_specs=out_specs, check_vma=False)
```

```python
import functools
import math

import jax
import jax.numpy as jnp
import numpy as np
from jax import lax
from jax.experimental import pallas as pl
from jax.experimental.pallas import tpu as pltpu
from jax.sharding import PartitionSpec as P


GY = 8
GZ = 4
LANES = 128
PACK = 1 << 16

F32 = jnp.float32
BF16 = jnp.bfloat16


def dot_nt(left, right):
    return lax.dot_general(left, right, (((1,), (1,)), ((), ())), preferred_element_type=F32)


def dot_nn(left, right):
    return lax.dot_general(left, right, (((1,), (0,)), ((), ())), preferred_element_type=F32)


def split(value):
    high = value.astype(BF16)
    return high, (value - high.astype(F32)).astype(BF16)


def plane_table(points_y, points_z):
    freq = np.arange(4 * GY * GZ)
    turns = np.outer(freq // (2 * GZ), points_y) % (2 * GY) / (2 * GY)
    turns = turns + np.outer(freq % (2 * GZ), points_z) % (2 * GZ) / (2 * GZ)
    cosine, sine = np.cos(2.0 * math.pi * turns), np.sin(2.0 * math.pi * turns)
    table = np.block([[cosine, sine], [-sine, cosine]]).astype(np.float32)
    high = table.astype(BF16)
    return high, (table - high.astype(np.float32)).astype(BF16)


def part_rows(box, rhs):
    start = 2 * box * rhs
    return slice(start, start + rhs), slice(start + rhs, start + 2 * rhs)


def encode_kernel(rhs, group, src_hbm, enc_hbm, out_ref, whole_ref, share_ref, src_ref, enc_ref, coded_ref, sem):
    copies = [
        pltpu.make_async_copy(src_hbm, src_ref, sem.at[0]),
        pltpu.make_async_copy(enc_hbm.at[0], enc_ref.at[0], sem.at[1]),
        pltpu.make_async_copy(enc_hbm.at[1], enc_ref.at[1], sem.at[2]),
    ]
    for copy in copies:
        copy.start()
    copies[0].wait()
    src = src_ref[...]
    whole_ref[...] = src
    part = src.shape[0] // lax.axis_size("dir")
    share_ref[...] = src_ref[pl.ds(pl.multiple_of(lax.axis_index("dir") * part, part), part), :]
    copies[1].wait()
    with_re = dot_nt(src, enc_ref[0])
    copies[2].wait()
    with_im = dot_nt(src, enc_ref[1])
    rows = src.shape[0] // rhs
    pieces = LANES // group
    for block in range(coded_ref.shape[0]):
        cols = slice(block * LANES, (block + 1) * LANES)
        for box in range(rows // 2):
            re, im = part_rows(box, rhs)
            coded_ref[block, re, :] = with_re[re, cols] - with_im[im, cols]
            coded_ref[block, im, :] = with_re[im, cols] + with_im[re, cols]
    for block in range(coded_ref.shape[0]):
        flat = coded_ref.at[block]
        for tile in range(rhs // pieces):
            parts = [flat[pl.ds(tile * pieces + n, rows, stride=rhs), :] for n in range(pieces)]
            for slot in range(pieces):
                lanes = slice(slot * group, (slot + 1) * group)
                out_ref[block * pieces + slot, :, tile * LANES : (tile + 1) * LANES] = jnp.concatenate(
                    [part[:, lanes] for part in parts], axis=1
                ).astype(BF16)


def table_kernel(
    grid_x, parts, share, list_hbm, mask_hbm, box_hbm, kern_hbm, cell_hbm, full_hbm,
    fwd_ref, inv_ref, spec_ref, order_ref, list_ref, mask_ref, box_ref, kern_ref, cell_ref, full_ref, sem,
):
    copies = [
        pltpu.make_async_copy(box_hbm, box_ref, sem.at[0]),
        pltpu.make_async_copy(cell_hbm, cell_ref, sem.at[1]),
        pltpu.make_async_copy(kern_hbm, kern_ref, sem.at[2]),
        pltpu.make_async_copy(full_hbm, full_ref, sem.at[3]),
        pltpu.make_async_copy(list_hbm, list_ref, sem.at[4]),
        pltpu.make_async_copy(mask_hbm, mask_ref, sem.at[5]),
    ]
    for copy in copies:
        copy.start()
    copies[4].wait()
    copies[5].wait()
    list_slots(share, list_ref[...], mask_ref[...], order_ref)
    full_hi, full_lo = full_ref.at[0], full_ref.at[1]
    cell_hi, cell_lo = cell_ref.at[0], cell_ref.at[1]
    plane = full_hi.shape[0] // 2
    cells = GY * GZ
    count = box_ref.shape[1]
    boxes = count * parts
    copies[0].wait()
    copies[1].wait()
    same = lax.broadcasted_iota(jnp.int32, (boxes, count), 0) // parts == lax.broadcasted_iota(jnp.int32, (boxes, count), 1)
    cell_col = jnp.sum(jnp.where(same, box_ref[...], 0), axis=1, keepdims=True)
    spread = jnp.where(same, 1.0, 0.0).astype(BF16)
    cell_row = dot_nt(jnp.broadcast_to(box_ref[...], (8, count)).astype(BF16), spread)[:1].astype(jnp.int32)
    down = lax.broadcasted_iota(jnp.int32, (2 * cells, boxes), 0)
    part_row = lax.broadcasted_iota(jnp.int32, (2 * cells, boxes), 1) % 2
    across = lax.broadcasted_iota(jnp.int32, (boxes, 2 * cells), 1)
    part_col = lax.broadcasted_iota(jnp.int32, (boxes, 2 * cells), 0) % 2
    for x in range(grid_x):
        hit = (cell_row - x * cells + part_row * cells == down) & (cell_row // cells == x)
        place = jnp.where(hit, 1.0, 0.0).astype(BF16)
        fwd_ref[x, :, :boxes] = dot_nn(cell_hi[...], place).astype(BF16)
        fwd_ref[x, :, boxes:] = dot_nn(cell_lo[...], place).astype(BF16)
        hit = (cell_col - x * cells + part_col * cells == across) & (cell_col // cells == x)
        place = jnp.where(hit, 1.0 / plane, 0.0).astype(BF16)
        inv_ref[x, 0] = dot_nt(place, cell_hi[...]).astype(BF16)
        inv_ref[x, 1] = dot_nt(place, cell_lo[...]).astype(BF16)
    point = lax.broadcasted_iota(jnp.int32, (1, 2 * plane), 1) % plane
    off_y, off_z = point // (2 * GZ), point % (2 * GZ)
    close = ((off_y <= 1) | (off_y == 2 * GY - 1)) & ((off_z <= 1) | (off_z == 2 * GZ - 1))
    keep = jnp.where(close, 0.0, 1.0)
    copies[2].wait()
    copies[3].wait()
    repeat = LANES // kern_ref.shape[0]
    double_x = kern_ref.shape[2]
    for off in range(double_x):
        if off == grid_x:
            continue
        kept = jnp.concatenate([kern_ref[:, 0, off, :], kern_ref[:, 1, off, :]], axis=1)
        if off <= 1 or off == double_x - 1:
            kept = kept * keep
        high, low = split(kept)
        high = jnp.concatenate([high] * repeat, axis=0)
        low = jnp.concatenate([low] * repeat, axis=0)
        spec_ref[off] = dot_nt(full_hi[...], high) + dot_nt(full_hi[...], low) + dot_nt(full_lo[...], high)
    if grid_x == 2:
        for off in (1, 3):
            spec_ref[off] = spec_ref[off] - spec_ref[0]


def times(pair, spec, plane):
    re, im = pair
    s_re, s_im = spec[:plane], spec[plane:]
    return re * s_re - im * s_im, re * s_im + im * s_re


def far_kernel(grid_x, coded_ref, fwd_ref, inv_ref, spec_ref, out_ref):
    owners, rows, width = coded_ref.shape
    plane = spec_ref.shape[1] // 2
    double_x = spec_ref.shape[0]
    step = min(2 * LANES, width)
    for start in range(0, width, step):
        cols = slice(start, start + step)
        coded = coded_ref[:, :, cols].reshape(owners * rows, step)
        coded = jnp.concatenate([coded, coded], axis=0)
        data = [dot_nn(fwd_ref[x], coded) for x in range(grid_x)]
        shared = []
        if grid_x == 2:
            for tile in range(step // LANES):
                lanes = slice(tile * LANES, (tile + 1) * LANES)
                first = data[0][:plane, lanes], data[0][plane:, lanes]
                second = data[1][:plane, lanes], data[1][plane:, lanes]
                base = times((first[0] + second[0], first[1] + second[1]), spec_ref[0], plane)
                below, above = times(second, spec_ref[3], plane), times(first, spec_ref[1], plane)
                shared.append([jnp.concatenate([base[0] + p[0], base[1] + p[1]], axis=0) for p in (below, above)])
        total = None
        for x in range(grid_x):
            tiles = []
            for tile in range(step // LANES):
                lanes = slice(tile * LANES, (tile + 1) * LANES)
                if grid_x == 2:
                    tiles.append(shared[tile][x])
                    continue
                re = im = None
                for s in range(grid_x):
                    off = (x - s) % double_x
                    s_re, s_im = spec_ref[off, :plane], spec_ref[off, plane:]
                    d_re, d_im = data[s][:plane, lanes], data[s][plane:, lanes]
                    p_re = d_re * s_re - d_im * s_im
                    p_im = d_re * s_im + d_im * s_re
                    re = p_re if re is None else re + p_re
                    im = p_im if im is None else im + p_im
                tiles.append(jnp.concatenate([re, im], axis=0))
            high, low = split(jnp.concatenate(tiles, axis=1))
            term = dot_nn(inv_ref[x, 0], high) + dot_nn(inv_ref[x, 0], low) + dot_nn(inv_ref[x, 1], high)
            total = term if total is None else total + term
        out_ref[:, :, cols] = total.astype(BF16).reshape(owners, rows, step)


def list_slots(share, near_list, near_mask, order_ref):
    boxes, slots = near_list.shape
    me, side = lax.axis_index("box"), lax.axis_index("dir")
    rest = lax.axis_size("box") // 4
    source = jnp.concatenate([near_list, near_list], axis=0)
    valid = jnp.concatenate([near_mask, near_mask], axis=0) != 0
    apart, place = (source // boxes) ^ me, source % boxes
    group, inner = apart // rest, apart % rest
    in_half, whole_share = place % share, group >= 2
    core = jnp.where(whole_share, 3 - group, place // share)
    entry = jnp.where(whole_share, share + place, in_half + jnp.where(group == 1, share + boxes, 0)) * rest + inner
    row = lax.broadcasted_iota(jnp.int32, source.shape, 0)
    used = jnp.where(valid & ((core == side) == (row < boxes)), 1, 0)
    rank = lax.broadcasted_iota(jnp.int32, order_ref.shape, 1)
    entry = entry + (row % boxes) * (slots * PACK)
    order = jnp.full_like(rank, boxes * slots * PACK)
    filled = jnp.zeros((2 * boxes, 1), jnp.int32)
    for slot in range(slots):
        here = used[:, slot : slot + 1]
        hit = (rank == filled) & (here != 0)
        order = jnp.where(hit, entry[:, slot : slot + 1] + slot * PACK, order)
        filled = filled + here
    order_ref[...] = jnp.where(rank == slots, filled, order)


def near_products(half, boxes, order_ref, src_ref, blk_ref, acc, arrived):
    count = blk_ref.shape[0] - 1
    slots = count // boxes

    def product(box, ranks):
        row = half * boxes + box
        packed = [order_ref[row, rank] for rank in ranks]
        places = [lax.div(entry, PACK) for entry in packed]
        sources = [lax.rem(entry, PACK) for entry in packed]
        vectors = jnp.concatenate([src_ref[n] for n in sources], axis=1)
        return [
            dot_nt(vectors, jnp.concatenate([blk_ref[place, part] for place in places], axis=1)) for part in range(2)
        ]

    first = min(5, slots)
    for box in range(boxes):
        arrived(box)
        acc[box, 0], acc[box, 1] = product(box, range(first))
    for start in range(first, slots, 3):
        for box in range(boxes):

            @pl.when(order_ref[half * boxes + box, slots] > start)
            def _():
                more = product(box, range(start, min(start + 3, slots)))
                acc[box, 0] += more[0]
                acc[box, 1] += more[1]


def near_mine_kernel(boxes, order_ref, src_ref, blocks_hbm, blk_ref, out_ref, acc, sem):
    count = blk_ref.shape[0] - 1
    slots = count // boxes

    def block_copy(half, box, rank):
        place = lax.div(order_ref[half * boxes + box, rank], PACK)
        return pltpu.make_async_copy(
            blocks_hbm.at[box, place - box * slots], blk_ref.at[place], sem.at[half * boxes + box]
        )

    for half in range(2):
        for box in range(boxes):

            @pl.loop(0, order_ref[half * boxes + box, slots])
            def _(rank):
                block_copy(half, box, rank).start()

    blk_ref[count] = jnp.zeros(blk_ref.shape[1:], BF16)

    def arrived(half, box):
        @pl.loop(0, order_ref[half * boxes + box, slots])
        def _(rank):
            block_copy(half, box, rank).wait()

    near_products(0, boxes, order_ref, src_ref, blk_ref, acc, functools.partial(arrived, 0))
    for box in range(boxes):
        rows_re, rows_im, re, im = near_rows(box, acc.shape[2] // 2)
        out_ref[rows_re, :] = acc[box, 0, re, :] - acc[box, 1, im, :]
        out_ref[rows_im, :] = acc[box, 0, im, :] + acc[box, 1, re, :]
    for box in range(boxes):
        arrived(1, box)


def near_theirs_kernel(boxes, order_ref, src_ref, blk_ref, base_ref, out_ref, acc):
    near_products(1, boxes, order_ref, src_ref, blk_ref, acc, lambda box: None)
    for box in range(boxes):
        rows_re, rows_im, re, im = near_rows(box, acc.shape[2] // 2)
        out_ref[rows_re, :] = base_ref[rows_re, :] + (acc[box, 0, re, :] - acc[box, 1, im, :])
        out_ref[rows_im, :] = base_ref[rows_im, :] + (acc[box, 0, im, :] + acc[box, 1, re, :])


def near_rows(box, half):
    return (*part_rows(box, half), slice(0, half), slice(half, 2 * half))


def decode_kernel(rhs, group, far_ref, dec_ref, near_ref, own_ref, other_ref, wide, total):
    _, rows, width = far_ref.shape
    pieces = LANES // group
    for block in range(wide.shape[0]):
        flat = wide.at[block]
        for tile in range(width // LANES):
            cols = slice(tile * LANES, (tile + 1) * LANES)
            parts = [far_ref[block * pieces + slot, :, cols].astype(F32) for slot in range(pieces)]
            for n in range(pieces):
                lanes = slice(n * group, (n + 1) * group)
                flat[pl.ds(tile * pieces + n, rows, stride=rhs), :] = jnp.concatenate(
                    [part[:, lanes] for part in parts], axis=1
                )
    fields = jnp.concatenate([wide[block].astype(BF16) for block in range(wide.shape[0])], axis=1)
    with_re = dot_nn(fields, dec_ref[0])
    with_im = dot_nn(fields, dec_ref[1])
    for box in range(rows // 2):
        re, im = part_rows(box, rhs)
        total[re, :] = near_ref[re, :] + (with_re[re] - with_im[im])
        total[im, :] = near_ref[im, :] + (with_re[im] + with_im[re])
    half = total.shape[1] // 2
    first = lax.axis_index("dir") == 0
    left, right = total[:, :half], total[:, half:]
    own_ref[...] = jnp.where(first, left, right)
    other_ref[...] = jnp.where(first, right, left)


def stack_kernel(*refs):
    for n, ref in enumerate(refs[:-1]):
        refs[-1][:, n] = ref[...]


def lay_kernel(*refs):
    start = 0
    for ref in refs[:-1]:
        refs[-1][start : start + ref.shape[0]] = ref[...]
        start += ref.shape[0]


def join(kernel, pieces, shape):
    return pl.pallas_call(
        kernel,
        out_shape=pltpu.VMEM(shape, pieces[0].dtype),
        in_specs=[vmem()] * len(pieces),
        out_specs=vmem(),
        compiler_params=budget(4),
        name="join",
    )(*pieces)


def gather_shares(boxes, share):
    size = lax.axis_size("box")
    rest = size // 4
    pairs = [(2 * i + core, 2 * (i ^ ((3 - core) * rest)) + core) for i in range(size) for core in range(2)]
    whole = lax.ppermute(boxes, ("box", "dir"), pairs)
    third = lax.ppermute(share, "box", [(i, i ^ rest) for i in range(size)])
    count = 2 * share.shape[0] + boxes.shape[0]
    held = join(lay_kernel, [share, whole, third], (count,) + share.shape[1:])
    while rest > 1:
        fan = 4 if rest % 4 == 0 else 2
        rest //= fan
        moved = [held]
        for delta in range(1, fan):
            moved.append(lax.ppermute(held, "box", [(i, i ^ (delta * rest)) for i in range(size)]))
        count *= fan
        held = join(stack_kernel, moved, (held.shape[0], fan) + share.shape[1:]).reshape((count,) + share.shape[1:])
    return held


def budget(mebibytes):
    return pltpu.CompilerParams(vmem_limit_bytes=mebibytes << 20)


def stay(array):
    return pltpu.with_memory_space_constraint(array, pltpu.HBM)


def vmem():
    return pl.BlockSpec(memory_space=pltpu.VMEM)


def smem():
    return pl.BlockSpec(memory_space=pltpu.SMEM)


def hbm():
    return pl.BlockSpec(memory_space=pltpu.HBM)


def whole_product(sources, encode, kernel, decode, near_blocks, near_list, near_mask, box_cell):
    owners, sides = lax.axis_size("box"), lax.axis_size("dir")
    per_box, parts, rhs, unknowns = sources.shape
    group_dirs, _, double_x, plane = kernel.shape
    side_dirs = encode.shape[1]
    grid_x = double_x // 2
    rows = per_box * parts
    width = rhs * group_dirs
    boxes = box_cell.shape[0]

    share = per_box // sides
    coded, own_boxes, own_share = pl.pallas_call(
        functools.partial(encode_kernel, rhs, group_dirs),
        out_shape=(
            pltpu.VMEM((owners, rows, width), BF16),
            pltpu.VMEM((per_box * parts * rhs, unknowns), BF16),
            pltpu.VMEM((share * parts * rhs, unknowns), BF16),
        ),
        in_specs=[hbm(), hbm()],
        out_specs=(vmem(),) * 3,
        scratch_shapes=[
            pltpu.VMEM((rows * rhs, unknowns), BF16),
            pltpu.VMEM(encode.shape, BF16),
            pltpu.VMEM((side_dirs // LANES, rows * rhs, LANES), F32),
            pltpu.SemaphoreType.DMA((3,)),
        ],
        compiler_params=budget(8),
        name="encode",
    )(stay(sources.reshape(rows * rhs, unknowns)), stay(encode))
    arrived = lax.all_to_all(coded, "box", split_axis=0, concat_axis=0, tiled=True)
    mine = gather_shares(own_boxes.reshape(per_box, parts * rhs, unknowns), own_share.reshape(share, parts * rhs, unknowns))
    theirs = lax.ppermute(mine, "dir", [(i, 1 - i) for i in range(sides)])

    cell = np.arange(GY * GZ)
    cell_hi, cell_lo = plane_table(cell // GZ, cell % GZ)
    point = np.arange(plane)
    full_hi, full_lo = plane_table(point // (2 * GZ), point % (2 * GZ))
    constants = (np.stack([cell_hi, cell_lo]), np.stack([full_hi, full_lo]))
    count = per_box * near_list.shape[1]
    forward, inverse, spectrum, order = pl.pallas_call(
        functools.partial(table_kernel, grid_x, parts, share),
        out_shape=(
            pltpu.VMEM((grid_x, 2 * plane, 2 * parts * boxes), BF16),
            pltpu.VMEM((grid_x, 2, parts * boxes, 2 * plane), BF16),
            pltpu.VMEM((double_x, 2 * plane, LANES), F32),
            jax.ShapeDtypeStruct((2 * per_box, LANES), jnp.int32),
        ),
        in_specs=[hbm()] * 6,
        out_specs=(vmem(),) * 4,
        scratch_shapes=[
            pltpu.VMEM(near_list.shape, jnp.int32),
            pltpu.VMEM(near_mask.shape, jnp.int32),
            pltpu.VMEM((1, boxes), jnp.int32),
            pltpu.VMEM(kernel.shape, F32),
            pltpu.VMEM(constants[0].shape, BF16),
            pltpu.VMEM(constants[1].shape, BF16),
            pltpu.SemaphoreType.DMA((6,)),
        ],
        compiler_params=budget(24),
        name="tables",
    )(stay(near_list), stay(near_mask), stay(box_cell[None, :]), stay(kernel), *[stay(jnp.asarray(table)) for table in constants])

    far = pl.pallas_call(
        functools.partial(far_kernel, grid_x),
        out_shape=pltpu.VMEM((owners, rows, width), BF16),
        in_specs=[vmem()] * 4,
        out_specs=vmem(),
        compiler_params=budget(8),
        name="far",
    )(arrived, forward, inverse, spectrum)
    returned = lax.all_to_all(far, "box", split_axis=0, concat_axis=0, tiled=True)


    near_acc = pltpu.VMEM((per_box, parts, parts * rhs, unknowns), F32)
    blocks, near_part = pl.pallas_call(
        functools.partial(near_mine_kernel, per_box),
        out_shape=(
            pltpu.VMEM((count + 1,) + near_blocks.shape[2:], BF16),
            pltpu.VMEM((rows * rhs, unknowns), F32),
        ),
        in_specs=[smem(), vmem(), hbm()],
        out_specs=(vmem(),) * 2,
        scratch_shapes=[near_acc, pltpu.SemaphoreType.DMA((2 * per_box,))],
        compiler_params=budget(4),
        name="near_mine",
    )(order, mine, stay(near_blocks))
    near_part = pl.pallas_call(
        functools.partial(near_theirs_kernel, per_box),
        out_shape=pltpu.VMEM((rows * rhs, unknowns), F32),
        in_specs=[smem(), vmem(), vmem(), vmem()],
        out_specs=vmem(),
        scratch_shapes=[near_acc],
        compiler_params=budget(4),
        name="near_theirs",
    )(order, theirs, blocks, near_part)

    half = unknowns // sides
    own, other = pl.pallas_call(
        functools.partial(decode_kernel, rhs, group_dirs),
        out_shape=(pltpu.VMEM((rows * rhs, half), F32),) * 2,
        in_specs=[vmem(), vmem(), vmem()],
        out_specs=(vmem(),) * 2,
        scratch_shapes=[
            pltpu.VMEM((side_dirs // LANES, rows * rhs, LANES), F32),
            pltpu.VMEM((rows * rhs, unknowns), F32),
        ],
        compiler_params=budget(8),
        name="decode",
    )(returned, decode, near_part)
    swapped = lax.ppermute(other, "dir", [(i, 1 - i) for i in range(sides)])
    return (own + swapped).reshape(per_box, parts, rhs, half)


def solution(mesh):
    in_specs = (
        P("box", None, None, None),
        P(None, "dir", None),
        P(("dir", "box"), None, None, None),
        P(None, "dir", None),
        P("box", "dir", None, None, None),
        P("box", "dir"),
        P("box", "dir"),
        P(),
    )
    out_specs = P("box", None, None, "dir")
    return jax.shard_map(whole_product, mesh=mesh, in_specs=in_specs, out_specs=out_specs, check_vma=False)
```
